32 devices in a mesh: dp: 8 (over z, x), tp: 4 (over y, core).
Axes of the slice: x: 2, y: 2, z: 4, core: 2. Of those that a mesh axis runs over, the one named last changes fastest.
Arguments:
- activations: bfloat16 [2048, 4096], P(('dp', 'tp')), may hold values from -700 to 700
- cotangent: bfloat16 [2048, 512], P('dp', 'tp'), may hold values from -6 to 6
- segment_ids: int32 [2048], P('dp'), may hold values from 0 to 31, never falling along the last dimension, each value on 1 to 128 neighbouring positions
- norm_gain: float32 [4096], replicated, may hold values from 0.5 to 1.5
- query_weight: bfloat16 [4096, 512], P(None, 'tp'), may hold values from -2 to 2
- key_value_weight: bfloat16 [4096, 512], P(None, 'tp'), may hold values from -1 to 1
Outputs:
- input_grad: bfloat16 [2048, 4096], P(('dp', 'tp'))
- query_grad: bfloat16 [4096, 512], P(None, 'tp')
- key_value_grad: bfloat16 [4096, 512], P(None, 'tp')
- gain_grad: float32 [4096], replicated
The draws below stay inside these ranges and needn't reach their ends.
Inputs may be any that keep to these rules, and one draw needn't show every extreme that they name: `segment_ids`: document numbers never fall along the tokens; a document has 1 to 128 tokens and may run on from one replica's rows into the next.
All inputs are finite; a program needn't handle non-finite values.
Results may differ from the reference program's by a relative error of at most 0.03.
Values may be sent and summed in bfloat16 or wider, within the bound.
A program may use at most 64 MiB of HBM per device.

```python
import math
import jax
import jax.numpy as jnp
import numpy as np
from jax import lax

D = 4096
HD = 128
TOK = 256
H = 4
KV = 2
ALLTOK = 2048
SEGS = 32
N_DP = 8


def base_keys(key):
    return jax.random.truncated_normal(jax.random.fold_in(key, 3), -4.0, 4.0, (D, KV, HD), jnp.float32)


def draw_query_weight(key, part):
    noise = jax.random.truncated_normal(jax.random.fold_in(key, 7), -4.0, 4.0, (D, H, HD), jnp.float32)
    weights = noise
    return jnp.clip(weights / math.sqrt(D), -2.0, 2.0).reshape(D, H * HD).astype(jnp.bfloat16)


def draw_key_value_weight(key, part):
    keys_part = base_keys(key)
    values_part = jax.random.truncated_normal(jax.random.fold_in(key, 5), -4.0, 4.0, (D, KV, HD), jnp.float32)
    return (jnp.stack([keys_part, values_part], axis=2) / math.sqrt(D)).reshape(D, KV * 2 * HD).astype(jnp.bfloat16)


def draw_activations(key, part):
    base = jax.random.truncated_normal(jax.random.fold_in(key, 11), -4.0, 4.0, (ALLTOK, D), jnp.float32)
    column_scale = jnp.exp(jax.random.uniform(jax.random.fold_in(key, 13), (1, D), jnp.float32, 0.0, math.log(10.0)))
    row_scale = jnp.exp(jax.random.uniform(jax.random.fold_in(key, 17), (ALLTOK, 1), jnp.float32, 0.0, math.log(10.0)))
    return (base * column_scale * row_scale).astype(jnp.bfloat16)


def shard_levels(rng, extent, split, low, largest):
    factor_of, own = 1.0, jax.random.fold_in(rng, 6)
    for axis_at, shards_of in split:
        steps = jnp.exp(jax.random.uniform(jax.random.fold_in(own, axis_at), (shards_of,), jnp.float32, low / len(split), largest / len(split)))
        factor_of = factor_of * jnp.repeat(steps, extent[axis_at] // shards_of).reshape([-1 if axis == axis_at else 1 for axis in range(len(extent))])
    return factor_of


def profile(number_of, total, most, skew):
    weights = [(1 << 20) // math.isqrt(grade ** skew) + 1 for grade in range(2, number_of + 1)]
    rest, holding = total - most - (number_of - 1), [1] * (number_of - 1)
    while rest > 0:
        candidates = [i for i in range(number_of - 1) if holding[i] < most]
        mass, remaining = sum([weights[i] for i in candidates]), rest
        for i in candidates:
            addition = min(most - holding[i], max(1, remaining * weights[i] // mass), rest)
            holding[i] = holding[i] + addition
            rest = rest - addition
    return np.array([most] + holding)


def ragged(key, number_of, total, most, skew):
    if number_of == 2:
        one = jax.random.randint(key, (), max(1, total - most), min(most, total - 1) + 1)
        return jnp.stack([one, total - one])
    lengths = jnp.asarray(profile(number_of, total, most, skew), jnp.int32)
    pairs = (number_of - 1) // 2
    source_of, taker = lengths[1:1 + 2 * pairs:2], lengths[2:2 + 2 * pairs:2]
    slack = jnp.minimum(source_of - 1, most - taker)
    moved = jax.random.randint(jax.random.fold_in(key, 1), (pairs,), 0, 1 << 20) % (slack + 1)
    lengths = lengths.at[1:1 + 2 * pairs:2].set(source_of - moved).at[2:2 + 2 * pairs:2].set(taker + moved)
    return lengths[jax.random.permutation(jax.random.fold_in(key, 2), number_of)]


def bell_draw(key, extent, deviation, most, pieces=(), kind=jnp.bfloat16):
    gain = shard_levels(key, extent, pieces, -0.22, 0.18) if pieces else 1.0
    result = jax.random.normal(key, extent, jnp.float32) * deviation * gain
    return jnp.minimum(jnp.maximum(result, -most), most).astype(kind)


def setup_inputs(seed: int = 0) -> dict:
    key_list = jax.random.split(jax.random.key(seed), 7)
    return {
        "activations": draw_activations(jax.random.fold_in(key_list[6], 71), 0),
        "cotangent": bell_draw(key_list[1], (ALLTOK, H * HD), 1.0, 6.0, ((0, 8), (1, 4))),
        "segment_ids": jnp.searchsorted(jnp.cumsum(ragged(key_list[2], SEGS, ALLTOK, TOK // 2, 1)), jnp.arange(ALLTOK), side="right").astype(jnp.int32),
        "norm_gain": jnp.clip(1.0 + 0.1 * jax.random.normal(key_list[3], (D,), jnp.float32), 0.5, 1.5),
        "query_weight": draw_query_weight(jax.random.fold_in(key_list[6], 71), 0),
        "key_value_weight": draw_key_value_weight(jax.random.fold_in(key_list[6], 71), 0),
    }


EPS = 1e-05

def rope_tables():
    position = jnp.arange(TOK, dtype=jnp.float32)
    frequency = 500000.0 ** (-jnp.arange(0, HD, 2, dtype=jnp.float32) / HD)
    angle = position[:, None] * frequency[None, :]
    return (jnp.cos(angle)[:, None, :], jnp.sin(angle)[:, None, :])

def rotate(values, cosine, sine):
    half = HD // 2
    first = values[..., :half]
    second = values[..., half:]
    return jnp.concatenate([first * cosine - second * sine, second * cosine + first * sine], axis=-1)

def replica(activations, cotangent, segment_ids, norm_gain, query_weight, key_value_weight):
    inputs_f = activations.astype(jnp.float32)
    root_mean = jnp.sqrt(lax.optimization_barrier(jnp.mean(inputs_f * inputs_f, axis=1, keepdims=True)) + EPS)
    unit_rows = inputs_f / root_mean
    normed = (unit_rows * norm_gain[None, :]).astype(jnp.bfloat16)
    cosine, sine = rope_tables()
    query_raw = jnp.dot(normed, query_weight, preferred_element_type=jnp.float32).reshape(TOK, H, HD)
    pair_raw = jnp.dot(normed, key_value_weight, preferred_element_type=jnp.float32).reshape(TOK, KV, 2, HD)
    query = rotate(query_raw, cosine, sine).astype(jnp.bfloat16)
    keys = rotate(pair_raw[:, :, 0], cosine, sine).astype(jnp.bfloat16)
    values = pair_raw[:, :, 1].astype(jnp.bfloat16)
    keys_heads = jnp.repeat(keys, 2, axis=1).astype(jnp.float32)
    values_heads = jnp.repeat(values, 2, axis=1).astype(jnp.float32)
    query_f = query.astype(jnp.float32)
    scale = HD ** (-0.5)
    position = jnp.arange(TOK)
    allowed = (position[:, None] >= position[None, :]) & (segment_ids[:, None] == segment_ids[None, :])
    scores = jnp.einsum('thd,shd->hts', query_f, keys_heads) * scale
    scores = jnp.where(allowed[None], scores, jnp.float32(-1e+30))
    top = lax.optimization_barrier(jnp.max(scores, axis=2, keepdims=True))
    exp_scores = jnp.exp(scores - top)
    probs = exp_scores / lax.optimization_barrier(jnp.sum(exp_scores, axis=2, keepdims=True))
    probs_half = probs.astype(jnp.bfloat16)
    cot_heads = cotangent.reshape(TOK, H, HD).astype(jnp.float32)
    prob_grad = jnp.einsum('thd,shd->hts', cot_heads, values_heads)
    delta = lax.optimization_barrier(jnp.sum(probs * prob_grad, axis=2, keepdims=True))
    score_grad = (probs * (prob_grad - delta) * scale).astype(jnp.bfloat16).astype(jnp.float32)
    query_back = jnp.einsum('hts,shd->thd', score_grad, keys_heads)
    keys_back = jnp.einsum('hts,thd->shd', score_grad, query_f)
    values_back = jnp.einsum('hts,thd->shd', probs_half.astype(jnp.float32), cot_heads)
    query_part = rotate(query_back, cosine, -sine).astype(jnp.bfloat16)
    key_part = rotate(keys_back, cosine, -sine).astype(jnp.bfloat16)
    value_part = values_back.astype(jnp.bfloat16)
    query_flat = query_part.reshape(TOK, H * HD)
    key_sum = key_part.astype(jnp.float32).reshape(TOK, KV, 2, HD).sum(axis=2)
    value_sum = value_part.astype(jnp.float32).reshape(TOK, KV, 2, HD).sum(axis=2)
    pair_grad = jnp.stack([key_sum, value_sum], axis=2).reshape(TOK, KV * 2 * HD)
    query_term = jnp.dot(normed.T, query_flat, preferred_element_type=jnp.float32).astype(jnp.bfloat16)
    pair_term = jnp.dot(normed.astype(jnp.float32).T, pair_grad, precision=lax.Precision.HIGHEST).astype(jnp.bfloat16)
    normed_grad = jnp.dot(query_flat, query_weight.T, preferred_element_type=jnp.float32)
    normed_grad = normed_grad + jnp.dot(pair_grad, key_value_weight.astype(jnp.float32).T, precision=lax.Precision.HIGHEST)
    gain_term = lax.optimization_barrier(jnp.sum(normed_grad * unit_rows, axis=0))
    scaled = normed_grad * norm_gain[None, :]
    inner = lax.optimization_barrier(jnp.mean(scaled * unit_rows, axis=1, keepdims=True))
    input_grad = ((scaled - unit_rows * inner) / root_mean).astype(jnp.bfloat16)
    return (input_grad, query_term, pair_term, gain_term)

def reference(activations, cotangent, segment_ids, norm_gain, query_weight, key_value_weight):
    acts = activations.reshape(N_DP, TOK, D)
    cots = cotangent.reshape(N_DP, TOK, H * HD)
    segs = segment_ids.reshape(N_DP, TOK)

    def step(carry, inputs):
        input_grad, query_term, pair_term, gain_term = replica(inputs[0], inputs[1], inputs[2], norm_gain, query_weight, key_value_weight)
        query_sum, pair_sum, gain_sum = carry
        carry = (query_sum + query_term.astype(jnp.float32), pair_sum + pair_term.astype(jnp.float32), gain_sum + gain_term)
        return (carry, input_grad)
    start = (jnp.zeros((D, H * HD), jnp.float32), jnp.zeros((D, KV * 2 * HD), jnp.float32), jnp.zeros((D,), jnp.float32))
    (query_sum, pair_sum, gain_sum), grads = lax.scan(step, start, (acts, cots, segs))
    return (grads.reshape(N_DP * TOK, D), query_sum.astype(jnp.bfloat16), pair_sum.astype(jnp.bfloat16), gain_sum)
```

```python
import functools

import jax
import jax.numpy as jnp
import numpy as np
from jax import lax
from jax.experimental import pallas as pl
from jax.experimental.pallas import tpu as pltpu
from jax.sharding import PartitionSpec as P

EPS = 1e-05
AG_CHUNKS = 4
DP_CHUNKS = 4
RS_CHUNKS = 4


def low_bit(d):
    return d & -d


def bits_of(n):
    return [1 << k for k in range(n.bit_length() - 1)]


def bit_at(v, b):
    return lax.rem(lax.div(v, b), 2)


def xor(v, mask):
    out = v
    for b in bits_of(1 << mask.bit_length()):
        if mask & b:
            out = out + b - 2 * b * bit_at(v, b)
    return out


def dot(a, b, ca, cb):
    return lax.dot_general(a, b, (((ca,), (cb,)), ((), ())), preferred_element_type=jnp.float32)


def kernel(ntp, ndp, x_ref, cot_ref, seg_ref, gain_ref, cos_ref, sin_ref, wq_ref, wkv_ref,
           ig_ref, qg_ref, kvg_ref, gg_ref,
           wcat, normed, grads, tot, rs_out, rs_in, term, halves, whole, gs, gr, kv_out, kv_in, inv_ref,
           w_sem, o_sem, ag_s, ag_r, rs_s, rs_r, dp_s, dp_r, g_s, g_r, kv_s, kv_r):
    tp, dp = lax.axis_index("tp"), lax.axis_index("dp")
    tp_bits, dp_bits = bits_of(ntp), bits_of(ndp)
    rows, width = x_ref.shape
    length = cot_ref.shape[0]
    head = cot_ref.shape[1]
    sends = []

    def remote(src, dst, s, r, axis, b):
        me = tp if axis == "tp" else dp
        return pltpu.make_async_remote_copy(
            src_ref=src, dst_ref=dst, send_sem=s, recv_sem=r,
            device_id={axis: xor(me, b)}, device_id_type=pl.DeviceIdType.MESH)

    def go(copy):
        copy.start()
        sends.append(copy)

    barrier = pltpu.get_barrier_semaphore()
    for b in tp_bits:
        pl.semaphore_signal(barrier, inc=1, device_id={"tp": xor(tp, b)},
                            device_id_type=pl.DeviceIdType.MESH)
    for b in dp_bits:
        pl.semaphore_signal(barrier, inc=1, device_id={"dp": xor(dp, b)},
                            device_id_type=pl.DeviceIdType.MESH)

    w_copies = [pltpu.make_async_copy(wq_ref, wcat.at[:, 0:head], w_sem.at[0]),
                pltpu.make_async_copy(wkv_ref, wcat.at[:, head:2 * head], w_sem.at[1])]
    for copy in w_copies:
        copy.start()

    def block(d):
        return pl.ds(pl.multiple_of(xor(tp, d) * rows, rows), rows)

    cw = width // AG_CHUNKS

    def cols(c, w=cw):
        return slice(c * w, (c + 1) * w)

    square = jnp.zeros((rows, 1), jnp.float32)
    for c in range(AG_CHUNKS):
        v = x_ref[:, cols(c)].astype(jnp.float32)
        square = square + jnp.sum(v * v, axis=1, keepdims=True)
    inv = 1.0 / jnp.sqrt(square * (1.0 / width) + EPS)
    inv_ref[...] = jnp.broadcast_to(inv, inv_ref.shape)

    def ag(c, d):
        b = low_bit(d)
        part = normed.at[block(d ^ b), cols(c)]
        return remote(part, part, ag_s.at[c, d], ag_r.at[c, d], "tp", b)

    order = sorted(range(1, ntp), key=lambda d: -low_bit(d))
    for c in range(AG_CHUNKS):
        unit = x_ref[:, cols(c)].astype(jnp.float32) * inv
        normed[block(0), cols(c)] = (unit * gain_ref[:, cols(c)]).astype(jnp.bfloat16)
        if c == 0:
            pl.semaphore_wait(barrier, len(tp_bits) + len(dp_bits))
        for b in reversed(tp_bits):
            go(ag(c, b))
    for copy in w_copies:
        copy.wait()
    proj = jnp.zeros((length, 2 * head), jnp.float32)

    def forward(c):
        for d in order:
            if low_bit(d) > 1:
                ag(c, d).wait_recv()
                for b in reversed(tp_bits):
                    if b < low_bit(d):
                        go(ag(c, d | b))

    def arrive(c, proj):
        for d in order:
            if low_bit(d) == 1:
                ag(c, d).wait_recv()
        return proj + dot(normed[:, cols(c)], wcat[cols(c), :], 1, 0)

    forward(0)
    for c in range(AG_CHUNKS):
        if c + 1 < AG_CHUNKS:
            forward(c + 1)
        proj = arrive(c, proj)

    odd = lax.rem(tp, 2) == 1
    cosine, sine = cos_ref[...], sin_ref[...]

    def rope(u):
        return u * cosine + pltpu.roll(u, head // 2, 1) * sine

    def rope_t(u):
        return u * cosine - pltpu.roll(u, head // 2, 1) * sine

    raw = proj[:, head:]
    own = jnp.where(odd, raw, rope(raw))
    kv_out[0] = own.astype(jnp.bfloat16)
    swap = remote(kv_out.at[0], kv_in.at[0], kv_s.at[0], kv_r.at[0], "tp", 1)
    go(swap)
    query = rope(proj[:, :head]).astype(jnp.bfloat16)
    seg_s = jnp.broadcast_to(seg_ref[...].astype(jnp.float32), (length, length))
    seg_t = seg_s.T
    t_at = lax.broadcasted_iota(jnp.int32, (length, length), 0)
    s_at = lax.broadcasted_iota(jnp.int32, (length, length), 1)
    allowed = (t_at >= s_at) & (seg_s == seg_t)
    scale = head ** (-0.5)
    swap.wait_recv()
    mine, other = kv_out[0].astype(jnp.float32), kv_in[0].astype(jnp.float32)
    keys = jnp.where(odd, other, mine).astype(jnp.bfloat16)
    values = jnp.where(odd, mine, other).astype(jnp.bfloat16)
    cot = cot_ref[...]
    scores = jnp.where(allowed, dot(query, keys, 1, 1) * scale, jnp.float32(-1e30))
    top = jnp.max(scores, axis=1, keepdims=True)
    e = jnp.exp(scores - top)
    probs = e / jnp.sum(e, axis=1, keepdims=True)
    prob_grad = dot(cot, values, 1, 1)
    delta = jnp.sum(probs * prob_grad, axis=1, keepdims=True)
    score_grad = (probs * (prob_grad - delta) * scale).astype(jnp.bfloat16)
    key_part = rope_t(dot(score_grad, query, 0, 0))
    value_part = dot(probs.astype(jnp.bfloat16), cot, 0, 0)
    kv_out[1] = jnp.where(odd, key_part, value_part).astype(jnp.bfloat16)
    swap = remote(kv_out.at[1], kv_in.at[1], kv_s.at[1], kv_r.at[1], "tp", 1)
    go(swap)
    own_grad = jnp.where(odd, value_part, key_part).astype(jnp.bfloat16).astype(jnp.float32)
    grads[:, :head] = rope_t(dot(score_grad, keys, 1, 0)).astype(jnp.bfloat16)
    swap.wait_recv()
    grads[:, head:] = (own_grad + kv_in[1].astype(jnp.float32)).astype(jnp.bfloat16)

    local = []

    def dp_task(q):
        bits = dp_bits if q % 2 == 0 else dp_bits[1:] + dp_bits[:1]
        nb = len(bits)
        size = width // DP_CHUNKS
        term[cols(q, size), :] = dot(normed[:, cols(q, size)], grads[...], 0, 0).astype(jnp.bfloat16)
        start, count, offset = q * size, size, 0
        starts = []
        copies = []
        for k, b in enumerate(bits):
            count = count // 2
            up = bit_at(dp, b)
            starts.append(start)
            away = pl.multiple_of(start + (1 - up) * count, count)
            keep = pl.multiple_of(start + up * count, count)
            land = halves.at[q, pl.ds(offset, count), :]
            copy = remote(term.at[pl.ds(away, count), :], land, dp_s.at[q, k], dp_r.at[q, k], "dp", b)
            go(copy)
            yield
            copy.wait_recv()
            summed = (term[pl.ds(keep, count), :].astype(jnp.float32)
                      + halves[q, pl.ds(offset, count), :].astype(jnp.float32)).astype(jnp.bfloat16)
            if k + 1 < nb:
                term[pl.ds(keep, count), :] = summed
            else:
                whole[pl.ds(keep, count), :] = summed
            start, offset = keep, offset + count
        for k in reversed(range(nb)):
            part = whole.at[pl.ds(start, count), :]
            copy = remote(part, part, dp_s.at[q, nb + k], dp_r.at[q, nb + k], "dp", bits[k])
            go(copy)
            yield
            copy.wait_recv()
            start, count = starts[k], count * 2
        for i, out in enumerate((qg_ref, kvg_ref)):
            copy = pltpu.make_async_copy(
                whole.at[cols(q, size), i * head:(i + 1) * head], out.at[cols(q, size), :], o_sem.at[q, i])
            copy.start()
            local.append(copy)

    rw = width // RS_CHUNKS
    rs_order = sorted(range(1, ntp), key=low_bit)

    def rs(c, d):
        return remote(rs_out.at[d, :, cols(c, rw)], rs_in.at[d, :, cols(c, rw)],
                      rs_s.at[c, d], rs_r.at[c, d], "tp", low_bit(d))

    def partial(c, d):
        value = tot[block(d), cols(c, rw)]
        for b in tp_bits:
            if d == 0 or b < low_bit(d):
                value = value + rs_in[d | b, :, cols(c, rw)].astype(jnp.float32)
        return value

    def rs_send(c, b):
        for d in rs_order:
            if low_bit(d) == b:
                rs_out[d, :, cols(c, rw)] = partial(c, d).astype(jnp.bfloat16)
                go(rs(c, d))

    def rs_wait(c, b):
        for d in rs_order:
            if low_bit(d) == b:
                rs(c, d).wait_recv()

    def tp_task():
        for c in range(RS_CHUNKS):
            tot[:, cols(c, rw)] = dot(grads[...], wcat[cols(c, rw), :], 1, 1)
            rs_send(c, 1)
        for b in tp_bits[1:]:
            for c in range(RS_CHUNKS):
                rs_wait(c, b // 2)
                rs_send(c, b)
        yield
        inner = jnp.zeros((rows, 1), jnp.float32)
        scale_back = inv_ref[:, 0:1]
        for c in range(RS_CHUNKS):
            rs_wait(c, tp_bits[-1])
            value = partial(c, 0)
            tot[block(0), cols(c, rw)] = value
            product = value * (x_ref[:, cols(c, rw)].astype(jnp.float32) * scale_back)
            gs[0, :, cols(c, rw)] = jnp.sum(product, axis=0, keepdims=True)
            inner = inner + jnp.sum(product * gain_ref[:, cols(c, rw)], axis=1, keepdims=True)
        rounds = [("tp", b) for b in tp_bits] + [("dp", b) for b in dp_bits]

        def exchange(k):
            axis, b = rounds[k]
            return remote(gs.at[k], gr.at[k], g_s.at[k], g_r.at[k], axis, b)

        go(exchange(0))
        inner = inner * (1.0 / width)
        for c in range(RS_CHUNKS):
            unit = x_ref[:, cols(c, rw)].astype(jnp.float32) * scale_back
            scaled = tot[block(0), cols(c, rw)] * gain_ref[:, cols(c, rw)]
            ig_ref[:, cols(c, rw)] = ((scaled - unit * inner) * scale_back).astype(jnp.bfloat16)
        for k in range(len(rounds)):
            yield
            exchange(k).wait_recv()
            if k + 1 < len(rounds):
                gs[k + 1] = gs[k] + gr[k]
                go(exchange(k + 1))
            else:
                gg_ref[...] = gs[k] + gr[k]

    tasks = [dp_task(q) for q in range(DP_CHUNKS)] + [tp_task()]
    while tasks:
        alive = []
        for task in tasks:
            try:
                next(task)
                alive.append(task)
            except StopIteration:
                pass
        tasks = alive
    for copy in local:
        copy.wait()
    for copy in sends:
        copy.wait_send()


def on_device(ntp, ndp, activations, cotangent, segment_ids, norm_gain, query_weight, key_value_weight):
    rows, width = activations.shape
    length, head = cotangent.shape
    angle = np.arange(length)[:, None] * 500000.0 ** (-np.arange(0, head, 2) / head)[None, :]
    cosine = np.concatenate([np.cos(angle), np.cos(angle)], axis=1).astype(np.float32)
    sine = np.concatenate([-np.sin(angle), np.sin(angle)], axis=1).astype(np.float32)
    nb = len(bits_of(ntp)) + len(bits_of(ndp))
    bf, f32 = jnp.bfloat16, jnp.float32
    vmem = pl.BlockSpec(memory_space=pltpu.VMEM)
    anywhere = pl.BlockSpec(memory_space=pl.ANY)
    dma = pltpu.SemaphoreType.DMA
    nd = len(bits_of(ndp))
    outs = pl.pallas_call(
        functools.partial(kernel, ntp, ndp),
        out_shape=[
            jax.ShapeDtypeStruct((rows, width), bf),
            jax.ShapeDtypeStruct((width, head), bf),
            jax.ShapeDtypeStruct((width, head), bf),
            jax.ShapeDtypeStruct((1, width), f32),
        ],
        in_specs=[vmem] * 6 + [anywhere] * 2,
        out_specs=[vmem, anywhere, anywhere, vmem],
        scratch_shapes=[
            pltpu.VMEM((width, 2 * head), bf),
            pltpu.VMEM((length, width), bf),
            pltpu.VMEM((length, 2 * head), bf),
            pltpu.VMEM((length, width), f32),
            pltpu.VMEM((ntp, rows, width), bf),
            pltpu.VMEM((ntp, rows, width), bf),
            pltpu.VMEM((width, 2 * head), bf),
            pltpu.VMEM((DP_CHUNKS, width // DP_CHUNKS, 2 * head), bf),
            pltpu.VMEM((width, 2 * head), bf),
            pltpu.VMEM((nb, 1, width), f32),
            pltpu.VMEM((nb, 1, width), f32),
            pltpu.VMEM((2, length, head), bf),
            pltpu.VMEM((2, length, head), bf),
            pltpu.VMEM((rows, 128), f32),
            dma((2,)),
            dma((DP_CHUNKS, 2)),
            dma((AG_CHUNKS, ntp)),
            dma((AG_CHUNKS, ntp)),
            dma((RS_CHUNKS, ntp)),
            dma((RS_CHUNKS, ntp)),
            dma((DP_CHUNKS, 2 * nd)),
            dma((DP_CHUNKS, 2 * nd)),
            dma((nb,)),
            dma((nb,)),
            dma((2,)),
            dma((2,)),
        ],
        compiler_params=pltpu.CompilerParams(
            collective_id=0, has_side_effects=True, vmem_limit_bytes=48 * 1024 * 1024),
    )(activations, cotangent, segment_ids.reshape(1, length), norm_gain.reshape(1, width),
      jnp.asarray(cosine), jnp.asarray(sine), query_weight, key_value_weight)
    return (outs[0], outs[1], outs[2], outs[3].reshape(width))


def solution(mesh):
    return jax.shard_map(
        functools.partial(on_device, mesh.shape["tp"], mesh.shape["dp"]),
        mesh=mesh,
        in_specs=(P(("dp", "tp"), None), P("dp", "tp"), P("dp"), P(), P(None, "tp"), P(None, "tp")),
        out_specs=(P(("dp", "tp"), None), P(None, "tp"), P(None, "tp"), P()),
        check_vma=False,
    )
```

```python
import functools

import jax
import jax.numpy as jnp
import numpy as np
from jax import lax
from jax.experimental import pallas as pl
from jax.experimental.pallas import tpu as pltpu
from jax.sharding import PartitionSpec as P

EPS = 1e-05
AG_CHUNKS = 4
DP_CHUNKS = 8
RS_CHUNKS = 4


def low_bit(d):
    return d & -d


def bits_of(n):
    return [1 << k for k in range(n.bit_length() - 1)]


def bit_at(v, b):
    return lax.rem(lax.div(v, b), 2)


def xor(v, mask):
    out = v
    for b in bits_of(1 << mask.bit_length()):
        if mask & b:
            out = out + b - 2 * b * bit_at(v, b)
    return out


def dot(a, b, ca, cb):
    return lax.dot_general(a, b, (((ca,), (cb,)), ((), ())), preferred_element_type=jnp.float32)


def kernel(ntp, ndp, x_ref, cot_ref, seg_ref, gain_ref, cos_ref, sin_ref, wq_ref, wkv_ref,
           ig_ref, qg_ref, kvg_ref, gg_ref,
           wcat, normed, normed_x, grads, grads_x, tot, rs_out, rs_in, term, chain, whole, gs, gr,
           kv_out, kv_in, inv_ref,
           w_sem, o_sem, ag_s, ag_r, nx_s, nx_r, gx_s, gx_r, rs_s, rs_r, in_s, in_r, down_s, down_r,
           last_s, last_r, g_s, g_r, kv_s, kv_r):
    tp, dp = lax.axis_index("tp"), lax.axis_index("dp")
    tp_bits, dp_bits = bits_of(ntp), bits_of(ndp)
    rows, width = x_ref.shape
    length = cot_ref.shape[0]
    head = cot_ref.shape[1]
    sends = []
    x, z, deep = lax.rem(dp, 2), lax.div(dp, 2), ndp // 2
    middle = deep // 2 - 1
    side = lax.div(z, deep // 2)
    depth = z + side * (deep - 1 - 2 * z)
    inner_dp = dp + 2 * (1 - 2 * side)
    outer_dp = dp - 2 * (1 - 2 * side)
    is_middle = lax.div(depth, middle) if middle else 1

    def to(src, dst, s, r, axis, device):
        return pltpu.make_async_remote_copy(
            src_ref=src, dst_ref=dst, send_sem=s, recv_sem=r,
            device_id={axis: device}, device_id_type=pl.DeviceIdType.MESH)

    def remote(src, dst, s, r, axis, b):
        return to(src, dst, s, r, axis, xor(tp if axis == "tp" else dp, b))

    def go(copy):
        copy.start()
        sends.append(copy)

    barrier = pltpu.get_barrier_semaphore()
    for b in tp_bits:
        pl.semaphore_signal(barrier, inc=1, device_id={"tp": xor(tp, b)},
                            device_id_type=pl.DeviceIdType.MESH)
    for b in dp_bits:
        pl.semaphore_signal(barrier, inc=1, device_id={"dp": xor(dp, b)},
                            device_id_type=pl.DeviceIdType.MESH)

    for step in (2, ndp - 2):
        pl.semaphore_signal(barrier, inc=1, device_id={"dp": lax.rem(dp + step, ndp)},
                            device_id_type=pl.DeviceIdType.MESH)

    w_copies = [pltpu.make_async_copy(wq_ref, wcat.at[:, 0:head], w_sem.at[0]),
                pltpu.make_async_copy(wkv_ref, wcat.at[:, head:2 * head], w_sem.at[1])]
    for copy in w_copies:
        copy.start()

    def block(d):
        return pl.ds(pl.multiple_of(xor(tp, d) * rows, rows), rows)

    cw = width // AG_CHUNKS

    def cols(c, w=cw):
        return slice(c * w, (c + 1) * w)

    square = jnp.zeros((rows, 1), jnp.float32)
    for c in range(AG_CHUNKS):
        v = x_ref[:, cols(c)].astype(jnp.float32)
        square = square + jnp.sum(v * v, axis=1, keepdims=True)
    inv = 1.0 / jnp.sqrt(square * (1.0 / width) + EPS)
    inv_ref[...] = jnp.broadcast_to(inv, inv_ref.shape)

    half = width // 2
    held = AG_CHUNKS // 2

    def turn(c):
        at = lax.rem(c + held * (1 - x), AG_CHUNKS) * cw
        return pl.ds(pl.multiple_of(at, cw), cw)

    def nx(c, d):
        if d & 1:
            part = normed_x.at[block(d ^ 1), cols(c)]
            return remote(part, part, nx_s.at[c, d], nx_r.at[c, d], "tp", 1)
        return remote(normed.at[block(d), turn(c)], normed_x.at[block(d), cols(c)],
                      nx_s.at[c, d], nx_r.at[c, d], "dp", 1)

    def ag(c, d):
        b = low_bit(d)
        part = normed.at[block(d ^ b), turn(c)]
        return remote(part, part, ag_s.at[c, d], ag_r.at[c, d], "tp", b)

    order = sorted(range(1, ntp), key=lambda d: -low_bit(d))
    for c in range(AG_CHUNKS):
        unit = x_ref[:, turn(c)].astype(jnp.float32) * inv
        normed[block(0), turn(c)] = (unit * gain_ref[:, turn(c)]).astype(jnp.bfloat16)
        if c == 0:
            pl.semaphore_wait(barrier, len(tp_bits) + len(dp_bits) + 2)
        for b in reversed(tp_bits):
            go(ag(c, b))
        if c < held:
            go(nx(c, 0))
    for copy in w_copies:
        copy.wait()
    proj = jnp.zeros((length, 2 * head), jnp.float32)

    def forward(c):
        for d in order:
            if low_bit(d) > 1:
                ag(c, d).wait_recv()
                for b in reversed(tp_bits):
                    if b < low_bit(d):
                        go(ag(c, d | b))
                if c < held:
                    go(nx(c, d))

    def arrive(c, proj):
        for d in order:
            if low_bit(d) == 1:
                ag(c, d).wait_recv()
        return proj + dot(normed[:, turn(c)], wcat[turn(c), :], 1, 0)

    forward(0)
    for c in range(AG_CHUNKS):
        if c + 1 < AG_CHUNKS:
            forward(c + 1)
        if c == AG_CHUNKS - 1:
            for i in range(held):
                for d in range(0, ntp, 2):
                    nx(i, d).wait_recv()
                    go(nx(i, d | 1))
        proj = arrive(c, proj)

    odd = lax.rem(tp, 2) == 1
    cosine, sine = cos_ref[...], sin_ref[...]

    def rope(u):
        return u * cosine + pltpu.roll(u, head // 2, 1) * sine

    def rope_t(u):
        return u * cosine - pltpu.roll(u, head // 2, 1) * sine

    raw = proj[:, head:]
    own = jnp.where(odd, raw, rope(raw))
    kv_out[0] = own.astype(jnp.bfloat16)
    swap = remote(kv_out.at[0], kv_in.at[0], kv_s.at[0], kv_r.at[0], "tp", 1)
    go(swap)
    query = rope(proj[:, :head]).astype(jnp.bfloat16)
    seg_s = jnp.broadcast_to(seg_ref[...].astype(jnp.float32), (length, length))
    seg_t = seg_s.T
    t_at = lax.broadcasted_iota(jnp.int32, (length, length), 0)
    s_at = lax.broadcasted_iota(jnp.int32, (length, length), 1)
    allowed = (t_at >= s_at) & (seg_s == seg_t)
    scale = head ** (-0.5)
    swap.wait_recv()
    mine, other = kv_out[0].astype(jnp.float32), kv_in[0].astype(jnp.float32)
    keys = jnp.where(odd, other, mine).astype(jnp.bfloat16)
    values = jnp.where(odd, mine, other).astype(jnp.bfloat16)
    cot = cot_ref[...]
    scores = jnp.where(allowed, dot(query, keys, 1, 1) * scale, jnp.float32(-1e30))
    top = jnp.max(scores, axis=1, keepdims=True)
    e = jnp.exp(scores - top)
    probs = e / jnp.sum(e, axis=1, keepdims=True)
    prob_grad = dot(cot, values, 1, 1)
    delta = jnp.sum(probs * prob_grad, axis=1, keepdims=True)
    score_grad = (probs * (prob_grad - delta) * scale).astype(jnp.bfloat16)
    key_part = rope_t(dot(score_grad, query, 0, 0))
    value_part = dot(probs.astype(jnp.bfloat16), cot, 0, 0)
    kv_out[1] = jnp.where(odd, key_part, value_part).astype(jnp.bfloat16)
    swap = remote(kv_out.at[1], kv_in.at[1], kv_s.at[1], kv_r.at[1], "tp", 1)
    go(swap)
    own_grad = jnp.where(odd, value_part, key_part).astype(jnp.bfloat16).astype(jnp.float32)
    grads[:, :head] = rope_t(dot(score_grad, keys, 1, 0)).astype(jnp.bfloat16)
    swap.wait_recv()
    grads[:, head:] = (own_grad + kv_in[1].astype(jnp.float32)).astype(jnp.bfloat16)

    send_grads = remote(grads, grads_x, gx_s, gx_r, "dp", 1)
    go(send_grads)

    local = []
    size = half // DP_CHUNKS

    def mine_rows(q):
        return pl.ds(pl.multiple_of(x * half + q * size, size), size)

    def other_rows(q):
        return pl.ds(pl.multiple_of((1 - x) * half + q * size, size), size)

    def inward(q):
        return to(term.at[cols(q, size), :], chain.at[q, is_middle], in_s.at[q], in_r.at[q, is_middle],
                  "dp", inner_dp)

    def arrived(q, slot):
        return to(term.at[cols(q, size), :], chain.at[q, slot], in_s.at[q], in_r.at[q, slot], "dp", inner_dp)

    def outward(q):
        part = whole.at[mine_rows(q), :]
        return to(part, part, down_s.at[q], down_r.at[q], "dp", outer_dp)

    def final(q):
        part = whole.at[mine_rows(q), :]
        return remote(part, part, last_s.at[q], last_r.at[q], "dp", 1)

    def save(q, upper):
        for i, out in enumerate((qg_ref, kvg_ref)):
            at = other_rows(q) if upper else mine_rows(q)
            copy = pltpu.make_async_copy(
                whole.at[at, i * head:(i + 1) * head], out.at[at, :], o_sem.at[q, 2 * upper + i])
            copy.start()
            local.append(copy)

    def form(q):
        own = dot(normed[:, mine_rows(q)], grads[...], 0, 0)
        value = own + dot(normed_x[:, cols(q, size)], grads_x[...], 0, 0)
        term[cols(q, size), :] = value.astype(jnp.bfloat16)

        @pl.when(depth == 0)
        def _():
            inward(q).start()

    def gather(q):
        @pl.when(depth > 0)
        def _():
            arrived(q, 0).wait_recv()
            term[cols(q, size), :] = (term[cols(q, size), :].astype(jnp.float32)
                                      + chain[q, 0].astype(jnp.float32)).astype(jnp.bfloat16)
            inward(q).start()

    def finish(q):
        @pl.when(depth == middle)
        def _():
            arrived(q, 1).wait_recv()
            whole[mine_rows(q), :] = (term[cols(q, size), :].astype(jnp.float32)
                                      + chain[q, 1].astype(jnp.float32)).astype(jnp.bfloat16)

        @pl.when(depth < middle)
        def _():
            outward(q).wait_recv()

        @pl.when(depth > 0)
        def _():
            outward(q).start()

        go(final(q))
        save(q, 0)

    def end(q):
        final(q).wait_recv()
        save(q, 1)

    rw = width // RS_CHUNKS
    rs_order = sorted(range(1, ntp), key=low_bit)

    def rs(c, d):
        return remote(rs_out.at[d, :, cols(c, rw)], rs_in.at[d, :, cols(c, rw)],
                      rs_s.at[c, d], rs_r.at[c, d], "tp", low_bit(d))

    def partial(c, d):
        value = tot[block(d), cols(c, rw)]
        for b in tp_bits:
            if d == 0 or b < low_bit(d):
                value = value + rs_in[d | b, :, cols(c, rw)].astype(jnp.float32)
        return value

    def rs_send(c, b):
        for d in rs_order:
            if low_bit(d) == b:
                rs_out[d, :, cols(c, rw)] = partial(c, d).astype(jnp.bfloat16)
                go(rs(c, d))

    def rs_wait(c, b):
        for d in rs_order:
            if low_bit(d) == b:
                rs(c, d).wait_recv()

    def tp_task():
        for c in range(RS_CHUNKS):
            tot[:, cols(c, rw)] = dot(grads[...], wcat[cols(c, rw), :], 1, 1)
            rs_send(c, 1)
        yield
        for b in tp_bits[1:]:
            for c in range(RS_CHUNKS):
                rs_wait(c, b // 2)
                rs_send(c, b)
        yield
        inner = jnp.zeros((rows, 1), jnp.float32)
        scale_back = inv_ref[:, 0:1]
        for c in range(RS_CHUNKS):
            rs_wait(c, tp_bits[-1])
            value = partial(c, 0)
            tot[block(0), cols(c, rw)] = value
            product = value * (x_ref[:, cols(c, rw)].astype(jnp.float32) * scale_back)
            gs[0, :, cols(c, rw)] = jnp.sum(product, axis=0, keepdims=True)
            inner = inner + jnp.sum(product * gain_ref[:, cols(c, rw)], axis=1, keepdims=True)
        rounds = [("tp", b) for b in tp_bits] + [("dp", b) for b in dp_bits]

        def exchange(k):
            axis, b = rounds[k]
            return remote(gs.at[k], gr.at[k], g_s.at[k], g_r.at[k], axis, b)

        go(exchange(0))
        inner = inner * (1.0 / width)
        for c in range(RS_CHUNKS):
            unit = x_ref[:, cols(c, rw)].astype(jnp.float32) * scale_back
            scaled = tot[block(0), cols(c, rw)] * gain_ref[:, cols(c, rw)]
            ig_ref[:, cols(c, rw)] = ((scaled - unit * inner) * scale_back).astype(jnp.bfloat16)
        for k in range(len(rounds)):
            yield
            exchange(k).wait_recv()
            if k + 1 < len(rounds):
                gs[k + 1] = gs[k] + gr[k]
                go(exchange(k + 1))
            else:
                gg_ref[...] = gs[k] + gr[k]

    task = tp_task()
    next(task)
    send_grads.wait_recv()
    for i in range(held):
        for d in range(0, ntp, 2):
            nx(i, d | 1).wait_recv()
    for q in range(DP_CHUNKS):
        form(q)
    next(task)
    for step in range(DP_CHUNKS + 3):
        for lag, stage in enumerate((gather, finish, end)):
            if 0 <= step - lag < DP_CHUNKS:
                stage(step - lag)
        next(task, None)
    for _ in task:
        pass
    for copy in local:
        copy.wait()
    for copy in sends:
        copy.wait_send()
    for q in range(DP_CHUNKS):
        inward(q).wait_send()

    @pl.when(depth > 0)
    def _():
        for q in range(DP_CHUNKS):
            outward(q).wait_send()


def on_device(ntp, ndp, activations, cotangent, segment_ids, norm_gain, query_weight, key_value_weight):
    rows, width = activations.shape
    length, head = cotangent.shape
    angle = np.arange(length)[:, None] * 500000.0 ** (-np.arange(0, head, 2) / head)[None, :]
    cosine = np.concatenate([np.cos(angle), np.cos(angle)], axis=1).astype(np.float32)
    sine = np.concatenate([-np.sin(angle), np.sin(angle)], axis=1).astype(np.float32)
    nb = len(bits_of(ntp)) + len(bits_of(ndp))
    bf, f32 = jnp.bfloat16, jnp.float32
    vmem = pl.BlockSpec(memory_space=pltpu.VMEM)
    anywhere = pl.BlockSpec(memory_space=pl.ANY)
    dma = pltpu.SemaphoreType.DMA
    outs = pl.pallas_call(
        functools.partial(kernel, ntp, ndp),
        out_shape=[
            jax.ShapeDtypeStruct((rows, width), bf),
            jax.ShapeDtypeStruct((width, head), bf),
            jax.ShapeDtypeStruct((width, head), bf),
            jax.ShapeDtypeStruct((1, width), f32),
        ],
        in_specs=[vmem] * 6 + [anywhere] * 2,
        out_specs=[vmem, anywhere, anywhere, vmem],
        scratch_shapes=[
            pltpu.VMEM((width, 2 * head), bf),
            pltpu.VMEM((length, width), bf),
            pltpu.VMEM((length, width // 2), bf),
            pltpu.VMEM((length, 2 * head), bf),
            pltpu.VMEM((length, 2 * head), bf),
            pltpu.VMEM((length, width), f32),
            pltpu.VMEM((ntp, rows, width), bf),
            pltpu.VMEM((ntp, rows, width), bf),
            pltpu.VMEM((width // 2, 2 * head), bf),
            pltpu.VMEM((DP_CHUNKS, 2, width // 2 // DP_CHUNKS, 2 * head), bf),
            pltpu.VMEM((width, 2 * head), bf),
            pltpu.VMEM((nb, 1, width), f32),
            pltpu.VMEM((nb, 1, width), f32),
            pltpu.VMEM((2, length, head), bf),
            pltpu.VMEM((2, length, head), bf),
            pltpu.VMEM((rows, 128), f32),
            dma((2,)),
            dma((DP_CHUNKS, 4)),
            dma((AG_CHUNKS, ntp)),
            dma((AG_CHUNKS, ntp)),
            dma((AG_CHUNKS // 2, ntp)),
            dma((AG_CHUNKS // 2, ntp)),
            dma,
            dma,
            dma((RS_CHUNKS, ntp)),
            dma((RS_CHUNKS, ntp)),
            dma((DP_CHUNKS,)),
            dma((DP_CHUNKS, 2)),
            dma((DP_CHUNKS,)),
            dma((DP_CHUNKS,)),
            dma((DP_CHUNKS,)),
            dma((DP_CHUNKS,)),
            dma((nb,)),
            dma((nb,)),
            dma((2,)),
            dma((2,)),
        ],
        compiler_params=pltpu.CompilerParams(
            collective_id=0, has_side_effects=True, vmem_limit_bytes=60 * 1024 * 1024),
    )(activations, cotangent, segment_ids.reshape(1, length), norm_gain.reshape(1, width),
      jnp.asarray(cosine), jnp.asarray(sine), query_weight, key_value_weight)
    return (outs[0], outs[1], outs[2], outs[3].reshape(width))


def solution(mesh):
    return jax.shard_map(
        functools.partial(on_device, mesh.shape["tp"], mesh.shape["dp"]),
        mesh=mesh,
        in_specs=(P(("dp", "tp"), None), P("dp", "tp"), P("dp"), P(), P(None, "tp"), P(None, "tp")),
        out_specs=(P(("dp", "tp"), None), P(None, "tp"), P(None, "tp"), P()),
        check_vma=False,
    )
```

```python
import functools

import jax
import jax.numpy as jnp
import numpy as np
from jax import lax
from jax.experimental import pallas as pl
from jax.experimental.pallas import tpu as pltpu
from jax.sharding import PartitionSpec as P

EPS = 1e-05
AG_CHUNKS = 4
DP_CHUNKS = 8
LAGS = (0, 2, 4)
TASK_AT = 5
RS_CHUNKS = 4


def low_bit(d):
    return d & -d


def bits_of(n):
    return [1 << k for k in range(n.bit_length() - 1)]


def bit_at(v, b):
    return lax.rem(lax.div(v, b), 2)


def xor(v, mask):
    out = v
    for b in bits_of(1 << mask.bit_length()):
        if mask & b:
            out = out + b - 2 * b * bit_at(v, b)
    return out


def dot(a, b, ca, cb):
    return lax.dot_general(a, b, (((ca,), (cb,)), ((), ())), preferred_element_type=jnp.float32)


def kernel(ntp, ndp, x_hbm, cot_hbm, seg_hbm, gain_hbm, cos_hbm, sin_hbm, wq_ref, wkv_ref,
           ig_ref, qg_ref, kvg_ref, gg_ref,
           wcat, normed, normed_x, grads, grads_x, tot, rs_out, rs_in, term, chain, whole, gs, gr,
           kv_out, kv_in, inv_ref,
           w_sem, o_sem, ag_s, ag_r, nx_s, nx_r, gx_s, gx_r, rs_s, rs_r, in_s, in_r, down_s, down_r,
           last_s, last_r, g_s, g_r, kv_s, kv_r,
           x_ref, cot_ref, seg_ref, gain_ref, cos_ref, sin_ref, load_sem):
    tp, dp = lax.axis_index("tp"), lax.axis_index("dp")
    tp_bits, dp_bits = bits_of(ntp), bits_of(ndp)
    rows, width = x_ref.shape
    length = cot_ref.shape[0]
    head = cot_ref.shape[1]
    sends = []
    x, z, deep = lax.rem(dp, 2), lax.div(dp, 2), ndp // 2
    middle = deep // 2 - 1
    side = lax.div(z, deep // 2)
    depth = z + side * (deep - 1 - 2 * z)
    inner_dp = dp + 2 * (1 - 2 * side)
    outer_dp = dp - 2 * (1 - 2 * side)
    is_middle = lax.div(depth, middle) if middle else 1

    def to(src, dst, s, r, axis, device):
        return pltpu.make_async_remote_copy(
            src_ref=src, dst_ref=dst, send_sem=s, recv_sem=r,
            device_id={axis: device}, device_id_type=pl.DeviceIdType.MESH)

    def remote(src, dst, s, r, axis, b):
        return to(src, dst, s, r, axis, xor(tp if axis == "tp" else dp, b))

    def go(copy):
        copy.start()
        sends.append(copy)

    loads = [pltpu.make_async_copy(src, dst, load_sem.at[i]) for i, (src, dst) in enumerate((
        (x_hbm, x_ref), (gain_hbm, gain_ref), (cot_hbm, cot_ref), (seg_hbm, seg_ref),
        (cos_hbm, cos_ref), (sin_hbm, sin_ref)))]
    for copy in loads:
        copy.start()
    barrier = pltpu.get_barrier_semaphore()
    for b in tp_bits:
        pl.semaphore_signal(barrier, inc=1, device_id={"tp": xor(tp, b)},
                            device_id_type=pl.DeviceIdType.MESH)
    for b in dp_bits:
        pl.semaphore_signal(barrier, inc=1, device_id={"dp": xor(dp, b)},
                            device_id_type=pl.DeviceIdType.MESH)

    for step in (2, ndp - 2):
        pl.semaphore_signal(barrier, inc=1, device_id={"dp": lax.rem(dp + step, ndp)},
                            device_id_type=pl.DeviceIdType.MESH)

    w_copies = [pltpu.make_async_copy(wq_ref, wcat.at[:, 0:head], w_sem.at[0]),
                pltpu.make_async_copy(wkv_ref, wcat.at[:, head:2 * head], w_sem.at[1])]
    for copy in w_copies:
        copy.start()

    def block(d):
        return pl.ds(pl.multiple_of(xor(tp, d) * rows, rows), rows)

    cw = width // AG_CHUNKS

    def cols(c, w=cw):
        return slice(c * w, (c + 1) * w)

    for copy in loads:
        copy.wait()
    square = jnp.zeros((rows, 1), jnp.float32)
    for c in range(AG_CHUNKS):
        v = x_ref[:, cols(c)].astype(jnp.float32)
        square = square + jnp.sum(v * v, axis=1, keepdims=True)
    inv = 1.0 / jnp.sqrt(square * (1.0 / width) + EPS)
    inv_ref[...] = jnp.broadcast_to(inv, inv_ref.shape)

    half = width // 2
    held = AG_CHUNKS // 2

    def turn(c):
        at = lax.rem(c + held * (1 - x), AG_CHUNKS) * cw
        return pl.ds(pl.multiple_of(at, cw), cw)

    def nx(c, d):
        if d & 1:
            part = normed_x.at[block(d ^ 1), cols(c)]
            return remote(part, part, nx_s.at[c, d], nx_r.at[c, d], "tp", 1)
        return remote(normed.at[block(d), turn(c)], normed_x.at[block(d), cols(c)],
                      nx_s.at[c, d], nx_r.at[c, d], "dp", 1)

    def ag(c, d):
        b = low_bit(d)
        part = normed.at[block(d ^ b), turn(c)]
        return remote(part, part, ag_s.at[c, d], ag_r.at[c, d], "tp", b)

    order = sorted(range(1, ntp), key=lambda d: -low_bit(d))
    for c in range(AG_CHUNKS):
        unit = x_ref[:, turn(c)].astype(jnp.float32) * inv
        normed[block(0), turn(c)] = (unit * gain_ref[:, turn(c)]).astype(jnp.bfloat16)
        if c == 0:
            pl.semaphore_wait(barrier, len(tp_bits) + len(dp_bits) + 2)
        for b in reversed(tp_bits):
            go(ag(c, b))
        if c < held:
            go(nx(c, 0))
    for copy in w_copies:
        copy.wait()
    proj = jnp.zeros((length, 2 * head), jnp.float32)

    def forward(c):
        for d in order:
            if low_bit(d) > 1:
                ag(c, d).wait_recv()
                for b in reversed(tp_bits):
                    if b < low_bit(d):
                        go(ag(c, d | b))
                if c < held:
                    go(nx(c, d))

    def arrive(c, proj):
        for d in order:
            if low_bit(d) == 1:
                ag(c, d).wait_recv()
        return proj + dot(normed[:, turn(c)], wcat[turn(c), :], 1, 0)

    forward(0)
    for c in range(AG_CHUNKS):
        if c + 1 < AG_CHUNKS:
            forward(c + 1)
        if c == AG_CHUNKS - 1:
            for i in range(held):
                for d in range(0, ntp, 2):
                    nx(i, d).wait_recv()
                    go(nx(i, d | 1))
        proj = arrive(c, proj)

    odd = lax.rem(tp, 2) == 1
    cosine, sine = cos_ref[...], sin_ref[...]

    def rope(u):
        return u * cosine + pltpu.roll(u, head // 2, 1) * sine

    def rope_t(u):
        return u * cosine - pltpu.roll(u, head // 2, 1) * sine

    raw = proj[:, head:]
    own = jnp.where(odd, raw, rope(raw))
    kv_out[0] = own.astype(jnp.bfloat16)
    swap = remote(kv_out.at[0], kv_in.at[0], kv_s.at[0], kv_r.at[0], "tp", 1)
    go(swap)
    query = rope(proj[:, :head]).astype(jnp.bfloat16)
    seg_s = jnp.broadcast_to(seg_ref[...].astype(jnp.float32), (length, length))
    seg_t = seg_s.T
    t_at = lax.broadcasted_iota(jnp.int32, (length, length), 0)
    s_at = lax.broadcasted_iota(jnp.int32, (length, length), 1)
    allowed = (t_at >= s_at) & (seg_s == seg_t)
    scale = head ** (-0.5)
    swap.wait_recv()
    mine, other = kv_out[0].astype(jnp.float32), kv_in[0].astype(jnp.float32)
    keys = jnp.where(odd, other, mine).astype(jnp.bfloat16)
    values = jnp.where(odd, mine, other).astype(jnp.bfloat16)
    cot = cot_ref[...]
    scores = jnp.where(allowed, dot(query, keys, 1, 1) * scale, jnp.float32(-1e30))
    top = jnp.max(scores, axis=1, keepdims=True)
    e = jnp.exp(scores - top)
    probs = e / jnp.sum(e, axis=1, keepdims=True)
    prob_grad = dot(cot, values, 1, 1)
    delta = jnp.sum(probs * prob_grad, axis=1, keepdims=True)
    score_grad = (probs * (prob_grad - delta) * scale).astype(jnp.bfloat16)
    key_part = rope_t(dot(score_grad, query, 0, 0))
    value_part = dot(probs.astype(jnp.bfloat16), cot, 0, 0)
    kv_out[1] = jnp.where(odd, key_part, value_part).astype(jnp.bfloat16)
    swap = remote(kv_out.at[1], kv_in.at[1], kv_s.at[1], kv_r.at[1], "tp", 1)
    go(swap)
    own_grad = jnp.where(odd, value_part, key_part).astype(jnp.bfloat16).astype(jnp.float32)
    grads[:, :head] = rope_t(dot(score_grad, keys, 1, 0)).astype(jnp.bfloat16)
    swap.wait_recv()
    grads[:, head:] = (own_grad + kv_in[1].astype(jnp.float32)).astype(jnp.bfloat16)

    send_grads = remote(grads, grads_x, gx_s, gx_r, "dp", 1)
    go(send_grads)

    local = []
    size = half // DP_CHUNKS

    def mine_rows(q):
        return pl.ds(pl.multiple_of(x * half + q * size, size), size)

    def other_rows(q):
        return pl.ds(pl.multiple_of((1 - x) * half + q * size, size), size)

    def inward(q):
        return to(term.at[cols(q, size), :], chain.at[q, is_middle], in_s.at[q], in_r.at[q, is_middle],
                  "dp", inner_dp)

    def arrived(q, slot):
        return to(term.at[cols(q, size), :], chain.at[q, slot], in_s.at[q], in_r.at[q, slot], "dp", inner_dp)

    def outward(q):
        part = whole.at[mine_rows(q), :]
        return to(part, part, down_s.at[q], down_r.at[q], "dp", outer_dp)

    def final(q):
        part = whole.at[mine_rows(q), :]
        return remote(part, part, last_s.at[q], last_r.at[q], "dp", 1)

    def save(q, upper):
        for i, out in enumerate((qg_ref, kvg_ref)):
            at = other_rows(q) if upper else mine_rows(q)
            copy = pltpu.make_async_copy(
                whole.at[at, i * head:(i + 1) * head], out.at[at, :], o_sem.at[q, 2 * upper + i])
            copy.start()
            local.append(copy)

    def form(q):
        own = dot(normed[:, mine_rows(q)], grads[...], 0, 0)
        value = own + dot(normed_x[:, cols(q, size)], grads_x[...], 0, 0)
        term[cols(q, size), :] = value.astype(jnp.bfloat16)

        @pl.when(depth == 0)
        def _():
            inward(q).start()

    def gather(q):
        @pl.when(depth > 0)
        def _():
            arrived(q, 0).wait_recv()
            term[cols(q, size), :] = (term[cols(q, size), :].astype(jnp.float32)
                                      + chain[q, 0].astype(jnp.float32)).astype(jnp.bfloat16)
            inward(q).start()

    def finish(q):
        @pl.when(depth == middle)
        def _():
            arrived(q, 1).wait_recv()
            whole[mine_rows(q), :] = (term[cols(q, size), :].astype(jnp.float32)
                                      + chain[q, 1].astype(jnp.float32)).astype(jnp.bfloat16)

        @pl.when(depth < middle)
        def _():
            outward(q).wait_recv()

        @pl.when(depth > 0)
        def _():
            outward(q).start()

        go(final(q))
        save(q, 0)

    def end(q):
        final(q).wait_recv()
        save(q, 1)

    rw = width // RS_CHUNKS
    rs_order = sorted(range(1, ntp), key=low_bit)

    def rs(c, d):
        return remote(rs_out.at[d, :, cols(c, rw)], rs_in.at[d, :, cols(c, rw)],
                      rs_s.at[c, d], rs_r.at[c, d], "tp", low_bit(d))

    def partial(c, d):
        value = tot[block(d), cols(c, rw)]
        for b in tp_bits:
            if d == 0 or b < low_bit(d):
                value = value + rs_in[d | b, :, cols(c, rw)].astype(jnp.float32)
        return value

    def rs_send(c, b):
        for d in rs_order:
            if low_bit(d) == b:
                rs_out[d, :, cols(c, rw)] = partial(c, d).astype(jnp.bfloat16)
                go(rs(c, d))

    def rs_wait(c, b):
        for d in rs_order:
            if low_bit(d) == b:
                rs(c, d).wait_recv()

    def tp_task():
        for c in range(RS_CHUNKS):
            tot[:, cols(c, rw)] = dot(grads[...], wcat[cols(c, rw), :], 1, 1)
            rs_send(c, 1)
        yield
        for b in tp_bits[1:]:
            for c in range(RS_CHUNKS):
                rs_wait(c, b // 2)
                rs_send(c, b)
        yield
        inner = jnp.zeros((rows, 1), jnp.float32)
        scale_back = inv_ref[:, 0:1]
        for c in range(RS_CHUNKS):
            rs_wait(c, tp_bits[-1])
            value = partial(c, 0)
            tot[block(0), cols(c, rw)] = value
            product = value * (x_ref[:, cols(c, rw)].astype(jnp.float32) * scale_back)
            gs[0, :, cols(c, rw)] = jnp.sum(product, axis=0, keepdims=True)
            inner = inner + jnp.sum(product * gain_ref[:, cols(c, rw)], axis=1, keepdims=True)
        rounds = [("tp", b) for b in tp_bits] + [("dp", b) for b in dp_bits]

        def exchange(k):
            axis, b = rounds[k]
            return remote(gs.at[k], gr.at[k], g_s.at[k], g_r.at[k], axis, b)

        go(exchange(0))
        inner = inner * (1.0 / width)
        for c in range(RS_CHUNKS):
            unit = x_ref[:, cols(c, rw)].astype(jnp.float32) * scale_back
            scaled = tot[block(0), cols(c, rw)] * gain_ref[:, cols(c, rw)]
            ig_ref[:, cols(c, rw)] = ((scaled - unit * inner) * scale_back).astype(jnp.bfloat16)
        for k in range(len(rounds)):
            yield
            exchange(k).wait_recv()
            if k + 1 < len(rounds):
                gs[k + 1] = gs[k] + gr[k]
                go(exchange(k + 1))
            else:
                gg_ref[...] = gs[k] + gr[k]

    task = tp_task()
    next(task)
    send_grads.wait_recv()
    for i in range(held):
        for d in range(0, ntp, 2):
            nx(i, d | 1).wait_recv()
    for q in range(DP_CHUNKS):
        form(q)
    next(task)
    for step in range(DP_CHUNKS + LAGS[2]):
        for lag, stage in zip(LAGS, (gather, finish, end)):
            if 0 <= step - lag < DP_CHUNKS:
                stage(step - lag)
        if step >= TASK_AT:
            next(task, None)
    for _ in task:
        pass
    for copy in local:
        copy.wait()
    for copy in sends:
        copy.wait_send()
    for q in range(DP_CHUNKS):
        inward(q).wait_send()

    @pl.when(depth > 0)
    def _():
        for q in range(DP_CHUNKS):
            outward(q).wait_send()


def on_device(ntp, ndp, activations, cotangent, segment_ids, norm_gain, query_weight, key_value_weight):
    rows, width = activations.shape
    length, head = cotangent.shape
    angle = np.arange(length)[:, None] * 500000.0 ** (-np.arange(0, head, 2) / head)[None, :]
    cosine = np.concatenate([np.cos(angle), np.cos(angle)], axis=1).astype(np.float32)
    sine = np.concatenate([-np.sin(angle), np.sin(angle)], axis=1).astype(np.float32)
    nb = len(bits_of(ntp)) + len(bits_of(ndp))
    bf, f32 = jnp.bfloat16, jnp.float32
    vmem = pl.BlockSpec(memory_space=pltpu.VMEM)
    anywhere = pl.BlockSpec(memory_space=pl.ANY)
    hbm = pl.BlockSpec(memory_space=pltpu.HBM)
    dma = pltpu.SemaphoreType.DMA
    outs = pl.pallas_call(
        functools.partial(kernel, ntp, ndp),
        out_shape=[
            jax.ShapeDtypeStruct((rows, width), bf),
            jax.ShapeDtypeStruct((width, head), bf),
            jax.ShapeDtypeStruct((width, head), bf),
            jax.ShapeDtypeStruct((1, width), f32),
        ],
        in_specs=[hbm] * 8,
        out_specs=[vmem, anywhere, anywhere, vmem],
        scratch_shapes=[
            pltpu.VMEM((width, 2 * head), bf),
            pltpu.VMEM((length, width), bf),
            pltpu.VMEM((length, width // 2), bf),
            pltpu.VMEM((length, 2 * head), bf),
            pltpu.VMEM((length, 2 * head), bf),
            pltpu.VMEM((length, width), f32),
            pltpu.VMEM((ntp, rows, width), bf),
            pltpu.VMEM((ntp, rows, width), bf),
            pltpu.VMEM((width // 2, 2 * head), bf),
            pltpu.VMEM((DP_CHUNKS, 2, width // 2 // DP_CHUNKS, 2 * head), bf),
            pltpu.VMEM((width, 2 * head), bf),
            pltpu.VMEM((nb, 1, width), f32),
            pltpu.VMEM((nb, 1, width), f32),
            pltpu.VMEM((2, length, head), bf),
            pltpu.VMEM((2, length, head), bf),
            pltpu.VMEM((rows, 128), f32),
            dma((2,)),
            dma((DP_CHUNKS, 4)),
            dma((AG_CHUNKS, ntp)),
            dma((AG_CHUNKS, ntp)),
            dma((AG_CHUNKS // 2, ntp)),
            dma((AG_CHUNKS // 2, ntp)),
            dma,
            dma,
            dma((RS_CHUNKS, ntp)),
            dma((RS_CHUNKS, ntp)),
            dma((DP_CHUNKS,)),
            dma((DP_CHUNKS, 2)),
            dma((DP_CHUNKS,)),
            dma((DP_CHUNKS,)),
            dma((DP_CHUNKS,)),
            dma((DP_CHUNKS,)),
            dma((nb,)),
            dma((nb,)),
            dma((2,)),
            dma((2,)),
            pltpu.VMEM((rows, width), bf),
            pltpu.VMEM((length, head), bf),
            pltpu.VMEM((1, length), jnp.int32),
            pltpu.VMEM((1, width), f32),
            pltpu.VMEM((length, head), f32),
            pltpu.VMEM((length, head), f32),
            dma((6,)),
        ],
        compiler_params=pltpu.CompilerParams(
            collective_id=0, has_side_effects=True, vmem_limit_bytes=60 * 1024 * 1024),
    )(activations, cotangent, segment_ids.reshape(1, length), norm_gain.reshape(1, width),
      jnp.asarray(cosine), jnp.asarray(sine), query_weight, key_value_weight)
    return (outs[0], outs[1], outs[2], outs[3].reshape(width))


def solution(mesh):
    return jax.shard_map(
        functools.partial(on_device, mesh.shape["tp"], mesh.shape["dp"]),
        mesh=mesh,
        in_specs=(P(("dp", "tp"), None), P("dp", "tp"), P("dp"), P(), P(None, "tp"), P(None, "tp")),
        out_specs=(P(("dp", "tp"), None), P(None, "tp"), P(None, "tp"), P()),
        check_vma=False,
    )
```

```python
import functools

import jax
import jax.numpy as jnp
import numpy as np
from jax import lax
from jax.experimental import pallas as pl
from jax.experimental.pallas import tpu as pltpu
from jax.sharding import PartitionSpec as P

EPS = 1e-05
AG_CHUNKS = 4
DP_CHUNKS = 16
LAGS = (0, 3, 6)
TASK_AT = 8
RS_CHUNKS = 4


def low_bit(d):
    return d & -d


def bits_of(n):
    return [1 << k for k in range(n.bit_length() - 1)]


def bit_at(v, b):
    return lax.rem(lax.div(v, b), 2)


def xor(v, mask):
    out = v
    for b in bits_of(1 << mask.bit_length()):
        if mask & b:
            out = out + b - 2 * b * bit_at(v, b)
    return out


def dot(a, b, ca, cb):
    return lax.dot_general(a, b, (((ca,), (cb,)), ((), ())), preferred_element_type=jnp.float32)


def kernel(ntp, ndp, x_hbm, cot_hbm, seg_hbm, gain_hbm, cos_hbm, sin_hbm, wq_ref, wkv_ref,
           ig_ref, qg_ref, kvg_ref, gg_ref,
           wcat, normed, normed_x, grads, grads_x, tot, rs_out, rs_in, term, chain, whole, gs, gr,
           kv_out, kv_in, inv_ref,
           w_sem, o_sem, ag_s, ag_r, nx_s, nx_r, gx_s, gx_r, rs_s, rs_r, in_s, in_r, down_s, down_r,
           last_s, last_r, g_s, g_r, kv_s, kv_r,
           x_ref, cot_ref, seg_ref, gain_ref, cos_ref, sin_ref, load_sem):
    tp, dp = lax.axis_index("tp"), lax.axis_index("dp")
    tp_bits, dp_bits = bits_of(ntp), bits_of(ndp)
    rows, width = x_ref.shape
    length = cot_ref.shape[0]
    head = cot_ref.shape[1]
    sends = []
    x, z, deep = lax.rem(dp, 2), lax.div(dp, 2), ndp // 2
    middle = deep // 2 - 1
    side = lax.div(z, deep // 2)
    depth = z + side * (deep - 1 - 2 * z)
    inner_dp = dp + 2 * (1 - 2 * side)
    outer_dp = dp - 2 * (1 - 2 * side)
    is_middle = lax.div(depth, middle) if middle else 1

    def to(src, dst, s, r, axis, device):
        return pltpu.make_async_remote_copy(
            src_ref=src, dst_ref=dst, send_sem=s, recv_sem=r,
            device_id={axis: device}, device_id_type=pl.DeviceIdType.MESH)

    def remote(src, dst, s, r, axis, b):
        return to(src, dst, s, r, axis, xor(tp if axis == "tp" else dp, b))

    def go(copy):
        copy.start()
        sends.append(copy)

    loads = [pltpu.make_async_copy(src, dst, load_sem.at[i]) for i, (src, dst) in enumerate((
        (x_hbm, x_ref), (gain_hbm, gain_ref), (cot_hbm, cot_ref), (seg_hbm, seg_ref),
        (cos_hbm, cos_ref), (sin_hbm, sin_ref)))]
    for copy in loads:
        copy.start()
    barrier = pltpu.get_barrier_semaphore()
    for b in tp_bits:
        pl.semaphore_signal(barrier, inc=1, device_id={"tp": xor(tp, b)},
                            device_id_type=pl.DeviceIdType.MESH)
    for b in dp_bits:
        pl.semaphore_signal(barrier, inc=1, device_id={"dp": xor(dp, b)},
                            device_id_type=pl.DeviceIdType.MESH)

    for step in (2, ndp - 2):
        pl.semaphore_signal(barrier, inc=1, device_id={"dp": lax.rem(dp + step, ndp)},
                            device_id_type=pl.DeviceIdType.MESH)

    w_copies = [pltpu.make_async_copy(wq_ref, wcat.at[:, 0:head], w_sem.at[0]),
                pltpu.make_async_copy(wkv_ref, wcat.at[:, head:2 * head], w_sem.at[1])]
    for copy in w_copies:
        copy.start()

    def block(d):
        return pl.ds(pl.multiple_of(xor(tp, d) * rows, rows), rows)

    cw = width // AG_CHUNKS

    def cols(c, w=cw):
        return slice(c * w, (c + 1) * w)

    for copy in loads:
        copy.wait()
    square = jnp.zeros((rows, 1), jnp.float32)
    for c in range(AG_CHUNKS):
        v = x_ref[:, cols(c)].astype(jnp.float32)
        square = square + jnp.sum(v * v, axis=1, keepdims=True)
    inv = 1.0 / jnp.sqrt(square * (1.0 / width) + EPS)
    inv_ref[...] = jnp.broadcast_to(inv, inv_ref.shape)

    half = width // 2
    held = AG_CHUNKS // 2

    def turn(c):
        at = lax.rem(c + held * (1 - x), AG_CHUNKS) * cw
        return pl.ds(pl.multiple_of(at, cw), cw)

    def nx(c, d):
        if d & 1:
            part = normed_x.at[block(d ^ 1), cols(c)]
            return remote(part, part, nx_s.at[c, d], nx_r.at[c, d], "tp", 1)
        return remote(normed.at[block(d), turn(c)], normed_x.at[block(d), cols(c)],
                      nx_s.at[c, d], nx_r.at[c, d], "dp", 1)

    def ag(c, d):
        b = low_bit(d)
        part = normed.at[block(d ^ b), turn(c)]
        return remote(part, part, ag_s.at[c, d], ag_r.at[c, d], "tp", b)

    order = sorted(range(1, ntp), key=lambda d: -low_bit(d))
    for c in range(AG_CHUNKS):
        unit = x_ref[:, turn(c)].astype(jnp.float32) * inv
        normed[block(0), turn(c)] = (unit * gain_ref[:, turn(c)]).astype(jnp.bfloat16)
        if c == 0:
            pl.semaphore_wait(barrier, len(tp_bits) + len(dp_bits) + 2)
        for b in reversed(tp_bits):
            go(ag(c, b))
        if c < held:
            go(nx(c, 0))
    for copy in w_copies:
        copy.wait()
    proj = jnp.zeros((length, 2 * head), jnp.float32)

    def forward(c):
        for d in order:
            if low_bit(d) > 1:
                ag(c, d).wait_recv()
                for b in reversed(tp_bits):
                    if b < low_bit(d):
                        go(ag(c, d | b))
                if c < held:
                    go(nx(c, d))

    def arrive(c, proj):
        for d in order:
            if low_bit(d) == 1:
                ag(c, d).wait_recv()
        return proj + dot(normed[:, turn(c)], wcat[turn(c), :], 1, 0)

    forward(0)
    for c in range(AG_CHUNKS):
        if c + 1 < AG_CHUNKS:
            forward(c + 1)
        if c == AG_CHUNKS - 1:
            for i in range(held):
                for d in range(0, ntp, 2):
                    nx(i, d).wait_recv()
                    go(nx(i, d | 1))
        proj = arrive(c, proj)

    odd = lax.rem(tp, 2) == 1
    cosine, sine = cos_ref[...], sin_ref[...]

    def rope(u):
        return u * cosine + pltpu.roll(u, head // 2, 1) * sine

    def rope_t(u):
        return u * cosine - pltpu.roll(u, head // 2, 1) * sine

    raw = proj[:, head:]
    own = jnp.where(odd, raw, rope(raw))
    kv_out[0] = own.astype(jnp.bfloat16)
    swap = remote(kv_out.at[0], kv_in.at[0], kv_s.at[0], kv_r.at[0], "tp", 1)
    go(swap)
    query = rope(proj[:, :head]).astype(jnp.bfloat16)
    seg_s = jnp.broadcast_to(seg_ref[...].astype(jnp.float32), (length, length))
    seg_t = seg_s.T
    t_at = lax.broadcasted_iota(jnp.int32, (length, length), 0)
    s_at = lax.broadcasted_iota(jnp.int32, (length, length), 1)
    allowed = (t_at >= s_at) & (seg_s == seg_t)
    scale = head ** (-0.5)
    swap.wait_recv()
    mine, other = kv_out[0].astype(jnp.float32), kv_in[0].astype(jnp.float32)
    keys = jnp.where(odd, other, mine).astype(jnp.bfloat16)
    values = jnp.where(odd, mine, other).astype(jnp.bfloat16)
    cot = cot_ref[...]
    scores = jnp.where(allowed, dot(query, keys, 1, 1) * scale, jnp.float32(-1e30))
    top = jnp.max(scores, axis=1, keepdims=True)
    e = jnp.exp(scores - top)
    probs = e / jnp.sum(e, axis=1, keepdims=True)
    prob_grad = dot(cot, values, 1, 1)
    delta = jnp.sum(probs * prob_grad, axis=1, keepdims=True)
    score_grad = (probs * (prob_grad - delta) * scale).astype(jnp.bfloat16)
    key_part = rope_t(dot(score_grad, query, 0, 0))
    value_part = dot(probs.astype(jnp.bfloat16), cot, 0, 0)
    kv_out[1] = jnp.where(odd, key_part, value_part).astype(jnp.bfloat16)
    swap = remote(kv_out.at[1], kv_in.at[1], kv_s.at[1], kv_r.at[1], "tp", 1)
    go(swap)
    own_grad = jnp.where(odd, value_part, key_part).astype(jnp.bfloat16).astype(jnp.float32)
    grads[:, :head] = rope_t(dot(score_grad, keys, 1, 0)).astype(jnp.bfloat16)
    swap.wait_recv()
    grads[:, head:] = (own_grad + kv_in[1].astype(jnp.float32)).astype(jnp.bfloat16)

    send_grads = remote(grads, grads_x, gx_s, gx_r, "dp", 1)
    go(send_grads)

    local = []
    size = half // DP_CHUNKS

    def mine_rows(q):
        return pl.ds(pl.multiple_of(x * half + q * size, size), size)

    def other_rows(q):
        return pl.ds(pl.multiple_of((1 - x) * half + q * size, size), size)

    def inward(q):
        return to(term.at[cols(q, size), :], chain.at[q, is_middle], in_s.at[q], in_r.at[q, is_middle],
                  "dp", inner_dp)

    def arrived(q, slot):
        return to(term.at[cols(q, size), :], chain.at[q, slot], in_s.at[q], in_r.at[q, slot], "dp", inner_dp)

    def outward(q):
        part = whole.at[mine_rows(q), :]
        return to(part, part, down_s.at[q], down_r.at[q], "dp", outer_dp)

    def final(q):
        part = whole.at[mine_rows(q), :]
        return remote(part, part, last_s.at[q], last_r.at[q], "dp", 1)

    def save(q, upper):
        for i, out in enumerate((qg_ref, kvg_ref)):
            at = other_rows(q) if upper else mine_rows(q)
            copy = pltpu.make_async_copy(
                whole.at[at, i * head:(i + 1) * head], out.at[at, :], o_sem.at[q, 2 * upper + i])
            copy.start()
            local.append(copy)

    def form(q):
        own = dot(normed[:, mine_rows(q)], grads[...], 0, 0)
        value = own + dot(normed_x[:, cols(q, size)], grads_x[...], 0, 0)
        term[cols(q, size), :] = value.astype(jnp.bfloat16)

        @pl.when(depth == 0)
        def _():
            inward(q).start()

    def gather(q):
        @pl.when(depth > 0)
        def _():
            arrived(q, 0).wait_recv()
            term[cols(q, size), :] = (term[cols(q, size), :].astype(jnp.float32)
                                      + chain[q, 0].astype(jnp.float32)).astype(jnp.bfloat16)
            inward(q).start()

    def finish(q):
        @pl.when(depth == middle)
        def _():
            arrived(q, 1).wait_recv()
            whole[mine_rows(q), :] = (term[cols(q, size), :].astype(jnp.float32)
                                      + chain[q, 1].astype(jnp.float32)).astype(jnp.bfloat16)

        @pl.when(depth < middle)
        def _():
            outward(q).wait_recv()

        @pl.when(depth > 0)
        def _():
            outward(q).start()

        go(final(q))
        save(q, 0)

    def end(q):
        final(q).wait_recv()
        save(q, 1)

    rw = width // RS_CHUNKS
    rs_order = sorted(range(1, ntp), key=low_bit)

    def rs(c, d):
        return remote(rs_out.at[d, :, cols(c, rw)], rs_in.at[d, :, cols(c, rw)],
                      rs_s.at[c, d], rs_r.at[c, d], "tp", low_bit(d))

    def partial(c, d):
        value = tot[block(d), cols(c, rw)]
        for b in tp_bits:
            if d == 0 or b < low_bit(d):
                value = value + rs_in[d | b, :, cols(c, rw)].astype(jnp.float32)
        return value

    def rs_send(c, b):
        for d in rs_order:
            if low_bit(d) == b:
                rs_out[d, :, cols(c, rw)] = partial(c, d).astype(jnp.bfloat16)
                go(rs(c, d))

    def rs_wait(c, b):
        for d in rs_order:
            if low_bit(d) == b:
                rs(c, d).wait_recv()

    def tp_task():
        for c in range(RS_CHUNKS):
            tot[:, cols(c, rw)] = dot(grads[...], wcat[cols(c, rw), :], 1, 1)
            rs_send(c, 1)
        yield
        for b in tp_bits[1:]:
            for c in range(RS_CHUNKS):
                rs_wait(c, b // 2)
                rs_send(c, b)
        yield
        inner = jnp.zeros((rows, 1), jnp.float32)
        scale_back = inv_ref[:, 0:1]
        for c in range(RS_CHUNKS):
            rs_wait(c, tp_bits[-1])
            value = partial(c, 0)
            tot[block(0), cols(c, rw)] = value
            product = value * (x_ref[:, cols(c, rw)].astype(jnp.float32) * scale_back)
            gs[0, :, cols(c, rw)] = jnp.sum(product, axis=0, keepdims=True)
            inner = inner + jnp.sum(product * gain_ref[:, cols(c, rw)], axis=1, keepdims=True)
        rounds = [("tp", b) for b in tp_bits] + [("dp", b) for b in dp_bits]

        def exchange(k):
            axis, b = rounds[k]
            return remote(gs.at[k], gr.at[k], g_s.at[k], g_r.at[k], axis, b)

        go(exchange(0))
        inner = inner * (1.0 / width)
        for c in range(RS_CHUNKS):
            unit = x_ref[:, cols(c, rw)].astype(jnp.float32) * scale_back
            scaled = tot[block(0), cols(c, rw)] * gain_ref[:, cols(c, rw)]
            ig_ref[:, cols(c, rw)] = ((scaled - unit * inner) * scale_back).astype(jnp.bfloat16)
        for k in range(len(rounds)):
            yield
            exchange(k).wait_recv()
            if k + 1 < len(rounds):
                gs[k + 1] = gs[k] + gr[k]
                go(exchange(k + 1))
            else:
                gg_ref[...] = gs[k] + gr[k]

    task = tp_task()
    next(task)
    send_grads.wait_recv()
    for i in range(held):
        for d in range(0, ntp, 2):
            nx(i, d | 1).wait_recv()
    for q in range(DP_CHUNKS):
        form(q)
    next(task)
    for step in range(DP_CHUNKS + LAGS[2]):
        for lag, stage in zip(LAGS, (gather, finish, end)):
            if 0 <= step - lag < DP_CHUNKS:
                stage(step - lag)
        if step >= TASK_AT and (step - TASK_AT) % 2 == 0:
            next(task, None)
    for _ in task:
        pass
    for copy in local:
        copy.wait()
    for copy in sends:
        copy.wait_send()
    for q in range(DP_CHUNKS):
        inward(q).wait_send()

    @pl.when(depth > 0)
    def _():
        for q in range(DP_CHUNKS):
            outward(q).wait_send()


def on_device(ntp, ndp, activations, cotangent, segment_ids, norm_gain, query_weight, key_value_weight):
    rows, width = activations.shape
    length, head = cotangent.shape
    angle = np.arange(length)[:, None] * 500000.0 ** (-np.arange(0, head, 2) / head)[None, :]
    cosine = np.concatenate([np.cos(angle), np.cos(angle)], axis=1).astype(np.float32)
    sine = np.concatenate([-np.sin(angle), np.sin(angle)], axis=1).astype(np.float32)
    nb = len(bits_of(ntp)) + len(bits_of(ndp))
    bf, f32 = jnp.bfloat16, jnp.float32
    vmem = pl.BlockSpec(memory_space=pltpu.VMEM)
    anywhere = pl.BlockSpec(memory_space=pl.ANY)
    hbm = pl.BlockSpec(memory_space=pltpu.HBM)
    dma = pltpu.SemaphoreType.DMA
    outs = pl.pallas_call(
        functools.partial(kernel, ntp, ndp),
        out_shape=[
            jax.ShapeDtypeStruct((rows, width), bf),
            jax.ShapeDtypeStruct((width, head), bf),
            jax.ShapeDtypeStruct((width, head), bf),
            jax.ShapeDtypeStruct((1, width), f32),
        ],
        in_specs=[hbm] * 8,
        out_specs=[vmem, anywhere, anywhere, vmem],
        scratch_shapes=[
            pltpu.VMEM((width, 2 * head), bf),
            pltpu.VMEM((length, width), bf),
            pltpu.VMEM((length, width // 2), bf),
            pltpu.VMEM((length, 2 * head), bf),
            pltpu.VMEM((length, 2 * head), bf),
            pltpu.VMEM((length, width), f32),
            pltpu.VMEM((ntp, rows, width), bf),
            pltpu.VMEM((ntp, rows, width), bf),
            pltpu.VMEM((width // 2, 2 * head), bf),
            pltpu.VMEM((DP_CHUNKS, 2, width // 2 // DP_CHUNKS, 2 * head), bf),
            pltpu.VMEM((width, 2 * head), bf),
            pltpu.VMEM((nb, 1, width), f32),
            pltpu.VMEM((nb, 1, width), f32),
            pltpu.VMEM((2, length, head), bf),
            pltpu.VMEM((2, length, head), bf),
            pltpu.VMEM((rows, 128), f32),
            dma((2,)),
            dma((DP_CHUNKS, 4)),
            dma((AG_CHUNKS, ntp)),
            dma((AG_CHUNKS, ntp)),
            dma((AG_CHUNKS // 2, ntp)),
            dma((AG_CHUNKS // 2, ntp)),
            dma,
            dma,
            dma((RS_CHUNKS, ntp)),
            dma((RS_CHUNKS, ntp)),
            dma((DP_CHUNKS,)),
            dma((DP_CHUNKS, 2)),
            dma((DP_CHUNKS,)),
            dma((DP_CHUNKS,)),
            dma((DP_CHUNKS,)),
            dma((DP_CHUNKS,)),
            dma((nb,)),
            dma((nb,)),
            dma((2,)),
            dma((2,)),
            pltpu.VMEM((rows, width), bf),
            pltpu.VMEM((length, head), bf),
            pltpu.VMEM((1, length), jnp.int32),
            pltpu.VMEM((1, width), f32),
            pltpu.VMEM((length, head), f32),
            pltpu.VMEM((length, head), f32),
            dma((6,)),
        ],
        compiler_params=pltpu.CompilerParams(
            collective_id=0, has_side_effects=True, vmem_limit_bytes=60 * 1024 * 1024),
    )(activations, cotangent, segment_ids.reshape(1, length), norm_gain.reshape(1, width),
      jnp.asarray(cosine), jnp.asarray(sine), query_weight, key_value_weight)
    return (outs[0], outs[1], outs[2], outs[3].reshape(width))


def solution(mesh):
    return jax.shard_map(
        functools.partial(on_device, mesh.shape["tp"], mesh.shape["dp"]),
        mesh=mesh,
        in_specs=(P(("dp", "tp"), None), P("dp", "tp"), P("dp"), P(), P(None, "tp"), P(None, "tp")),
        out_specs=(P(("dp", "tp"), None), P(None, "tp"), P(None, "tp"), P()),
        check_vma=False,
    )
```

```python
import functools

import jax
import jax.numpy as jnp
import numpy as np
from jax import lax
from jax.experimental import pallas as pl
from jax.experimental.pallas import tpu as pltpu
from jax.sharding import PartitionSpec as P

EPS = 1e-05
AG_CHUNKS = 4
DP_CHUNKS = 16
LAGS = (0, 3, 6)
TASK_AT = 8
RS_CHUNKS = 4


def low_bit(d):
    return d & -d


def bits_of(n):
    return [1 << k for k in range(n.bit_length() - 1)]


def bit_at(v, b):
    return lax.rem(lax.div(v, b), 2)


def xor(v, mask):
    out = v
    for b in bits_of(1 << mask.bit_length()):
        if mask & b:
            out = out + b - 2 * b * bit_at(v, b)
    return out


def dot(a, b, ca, cb):
    return lax.dot_general(a, b, (((ca,), (cb,)), ((), ())), preferred_element_type=jnp.float32)


def kernel(ntp, ndp, x_hbm, cot_hbm, seg_hbm, gain_hbm, cos_hbm, sin_hbm, wq_ref, wkv_ref,
           ig_ref, qg_ref, kvg_ref, gg_ref,
           wcat, normed, normed_x, grads, grads_x, tot, rs_out, rs_in, term, chain, whole, gs, gr,
           kv_out, kv_in, inv_ref,
           w_sem, o_sem, ag_s, ag_r, nx_s, nx_r, gx_s, gx_r, rs_s, rs_r, in_s, in_r, down_s, down_r,
           last_s, last_r, g_s, g_r, kv_s, kv_r,
           x_ref, cot_ref, seg_ref, gain_ref, cos_ref, sin_ref, load_sem):
    tp, dp = lax.axis_index("tp"), lax.axis_index("dp")
    tp_bits, dp_bits = bits_of(ntp), bits_of(ndp)
    rows, width = x_ref.shape
    length = cot_ref.shape[0]
    head = cot_ref.shape[1]
    sends = []
    x, z, deep = lax.rem(dp, 2), lax.div(dp, 2), ndp // 2
    middle = deep // 2 - 1
    side = lax.div(z, deep // 2)
    depth = z + side * (deep - 1 - 2 * z)
    inner_dp = dp + 2 * (1 - 2 * side)
    outer_dp = dp - 2 * (1 - 2 * side)
    is_middle = lax.div(depth, middle) if middle else 1

    def to(src, dst, s, r, axis, device):
        return pltpu.make_async_remote_copy(
            src_ref=src, dst_ref=dst, send_sem=s, recv_sem=r,
            device_id={axis: device}, device_id_type=pl.DeviceIdType.MESH)

    def remote(src, dst, s, r, axis, b):
        return to(src, dst, s, r, axis, xor(tp if axis == "tp" else dp, b))

    def go(copy):
        copy.start()
        sends.append(copy)

    loads = [pltpu.make_async_copy(src, dst, load_sem.at[i]) for i, (src, dst) in enumerate((
        (x_hbm, x_ref), (gain_hbm, gain_ref), (cot_hbm, cot_ref), (seg_hbm, seg_ref),
        (cos_hbm, cos_ref), (sin_hbm, sin_ref)))]
    for copy in loads:
        copy.start()
    barrier = pltpu.get_barrier_semaphore()
    for b in tp_bits:
        pl.semaphore_signal(barrier, inc=1, device_id={"tp": xor(tp, b)},
                            device_id_type=pl.DeviceIdType.MESH)
    for b in dp_bits:
        pl.semaphore_signal(barrier, inc=1, device_id={"dp": xor(dp, b)},
                            device_id_type=pl.DeviceIdType.MESH)

    for step in (2, ndp - 2):
        pl.semaphore_signal(barrier, inc=1, device_id={"dp": lax.rem(dp + step, ndp)},
                            device_id_type=pl.DeviceIdType.MESH)

    w_copies = [pltpu.make_async_copy(wq_ref, wcat.at[:, 0:head], w_sem.at[0]),
                pltpu.make_async_copy(wkv_ref, wcat.at[:, head:2 * head], w_sem.at[1])]
    for copy in w_copies:
        copy.start()

    def block(d):
        return pl.ds(pl.multiple_of(xor(tp, d) * rows, rows), rows)

    cw = width // AG_CHUNKS

    def cols(c, w=cw):
        return slice(c * w, (c + 1) * w)

    for copy in loads:
        copy.wait()
    square = jnp.zeros((rows, 1), jnp.float32)
    for c in range(AG_CHUNKS):
        v = x_ref[:, cols(c)].astype(jnp.float32)
        square = square + jnp.sum(v * v, axis=1, keepdims=True)
    inv = 1.0 / jnp.sqrt(square * (1.0 / width) + EPS)
    inv_ref[...] = jnp.broadcast_to(inv, inv_ref.shape)

    half = width // 2
    held = AG_CHUNKS // 2

    def turn(c):
        at = lax.rem(c + held * (1 - x), AG_CHUNKS) * cw
        return pl.ds(pl.multiple_of(at, cw), cw)

    def nx(c, d):
        if d & 1:
            part = normed_x.at[block(d ^ 1), cols(c)]
            return remote(part, part, nx_s.at[c, d], nx_r.at[c, d], "tp", 1)
        return remote(normed.at[block(d), turn(c)], normed_x.at[block(d), cols(c)],
                      nx_s.at[c, d], nx_r.at[c, d], "dp", 1)

    def ag(c, d):
        b = low_bit(d)
        part = normed.at[block(d ^ b), turn(c)]
        return remote(part, part, ag_s.at[c, d], ag_r.at[c, d], "tp", b)

    order = sorted(range(1, ntp), key=lambda d: -low_bit(d))
    for c in range(AG_CHUNKS):
        unit = x_ref[:, turn(c)].astype(jnp.float32) * inv
        normed[block(0), turn(c)] = (unit * gain_ref[:, turn(c)]).astype(jnp.bfloat16)
        if c == 0:
            pl.semaphore_wait(barrier, len(tp_bits) + len(dp_bits) + 2)
        for b in reversed(tp_bits):
            go(ag(c, b))
        if c < held:
            go(nx(c, 0))
    for copy in w_copies:
        copy.wait()
    proj = jnp.zeros((length, 2 * head), jnp.float32)

    def forward(c):
        for d in order:
            if low_bit(d) > 1:
                ag(c, d).wait_recv()
                for b in reversed(tp_bits):
                    if b < low_bit(d):
                        go(ag(c, d | b))
                if c < held:
                    go(nx(c, d))

    def arrive(c, proj):
        for d in order:
            if low_bit(d) == 1:
                ag(c, d).wait_recv()
        return proj + dot(normed[:, turn(c)], wcat[turn(c), :], 1, 0)

    forward(0)
    for c in range(AG_CHUNKS):
        if c + 1 < AG_CHUNKS:
            forward(c + 1)
        if c == AG_CHUNKS - 1:
            for i in range(held):
                for d in range(0, ntp, 2):
                    nx(i, d).wait_recv()
                    go(nx(i, d | 1))
        proj = arrive(c, proj)

    odd = lax.rem(tp, 2) == 1
    cosine, sine = cos_ref[...], sin_ref[...]

    def rope(u):
        return u * cosine + pltpu.roll(u, head // 2, 1) * sine

    def rope_t(u):
        return u * cosine - pltpu.roll(u, head // 2, 1) * sine

    raw = proj[:, head:]
    own = jnp.where(odd, raw, rope(raw))
    kv_out[0] = own.astype(jnp.bfloat16)
    swap = remote(kv_out.at[0], kv_in.at[0], kv_s.at[0], kv_r.at[0], "tp", 1)
    go(swap)
    query = rope(proj[:, :head]).astype(jnp.bfloat16)
    seg_s = jnp.broadcast_to(seg_ref[...].astype(jnp.float32), (length, length))
    seg_t = seg_s.T
    t_at = lax.broadcasted_iota(jnp.int32, (length, length), 0)
    s_at = lax.broadcasted_iota(jnp.int32, (length, length), 1)
    allowed = (t_at >= s_at) & (seg_s == seg_t)
    scale = head ** (-0.5)
    swap.wait_recv()
    mine, other = kv_out[0].astype(jnp.float32), kv_in[0].astype(jnp.float32)
    keys = jnp.where(odd, other, mine).astype(jnp.bfloat16)
    values = jnp.where(odd, mine, other).astype(jnp.bfloat16)
    cot = cot_ref[...]
    scores = jnp.where(allowed, dot(query, keys, 1, 1) * scale, jnp.float32(-1e30))
    top = jnp.max(scores, axis=1, keepdims=True)
    e = jnp.exp(scores - top)
    probs = e / jnp.sum(e, axis=1, keepdims=True)
    prob_grad = dot(cot, values, 1, 1)
    delta = jnp.sum(probs * prob_grad, axis=1, keepdims=True)
    score_grad = (probs * (prob_grad - delta) * scale).astype(jnp.bfloat16)
    key_part = rope_t(dot(score_grad, query, 0, 0))
    value_part = dot(probs.astype(jnp.bfloat16), cot, 0, 0)
    kv_out[1] = jnp.where(odd, key_part, value_part).astype(jnp.bfloat16)
    swap = remote(kv_out.at[1], kv_in.at[1], kv_s.at[1], kv_r.at[1], "tp", 1)
    go(swap)
    own_grad = jnp.where(odd, value_part, key_part).astype(jnp.bfloat16).astype(jnp.float32)
    grads[:, :head] = rope_t(dot(score_grad, keys, 1, 0)).astype(jnp.bfloat16)
    swap.wait_recv()
    grads[:, head:] = (own_grad + kv_in[1].astype(jnp.float32)).astype(jnp.bfloat16)

    send_grads = remote(grads, grads_x, gx_s, gx_r, "dp", 1)
    go(send_grads)

    local = []
    size = half // DP_CHUNKS

    def mine_rows(q):
        return pl.ds(pl.multiple_of(x * half + q * size, size), size)

    def other_rows(q):
        return pl.ds(pl.multiple_of((1 - x) * half + q * size, size), size)

    def inward(q):
        return to(term.at[cols(q, size), :], chain.at[q, is_middle], in_s.at[q], in_r.at[q, is_middle],
                  "dp", inner_dp)

    def arrived(q, slot):
        return to(term.at[cols(q, size), :], chain.at[q, slot], in_s.at[q], in_r.at[q, slot], "dp", inner_dp)

    def outward(q):
        part = whole.at[mine_rows(q), :]
        return to(part, part, down_s.at[q], down_r.at[q], "dp", outer_dp)

    def final(q):
        part = whole.at[mine_rows(q), :]
        return remote(part, part, last_s.at[q], last_r.at[q], "dp", 1)

    def save(q, upper):
        for i, out in enumerate((qg_ref, kvg_ref)):
            at = other_rows(q) if upper else mine_rows(q)
            copy = pltpu.make_async_copy(
                whole.at[at, i * head:(i + 1) * head], out.at[at, :], o_sem.at[q, 2 * upper + i])
            copy.start()
            local.append(copy)

    def form(q):
        own = dot(normed[:, mine_rows(q)], grads[...], 0, 0)
        value = own + dot(normed_x[:, cols(q, size)], grads_x[...], 0, 0)
        term[cols(q, size), :] = value.astype(jnp.bfloat16)

        @pl.when(depth == 0)
        def _():
            inward(q).start()

    def gather(q):
        @pl.when(depth > 0)
        def _():
            arrived(q, 0).wait_recv()
            term[cols(q, size), :] = (term[cols(q, size), :].astype(jnp.float32)
                                      + chain[q, 0].astype(jnp.float32)).astype(jnp.bfloat16)
            inward(q).start()

    def finish(q):
        @pl.when(depth == middle)
        def _():
            arrived(q, 1).wait_recv()
            whole[mine_rows(q), :] = (term[cols(q, size), :].astype(jnp.float32)
                                      + chain[q, 1].astype(jnp.float32)).astype(jnp.bfloat16)

        @pl.when(depth < middle)
        def _():
            outward(q).wait_recv()

        @pl.when(depth > 0)
        def _():
            outward(q).start()

        go(final(q))
        save(q, 0)

    def end(q):
        final(q).wait_recv()
        save(q, 1)

    rw = width // RS_CHUNKS
    rs_order = sorted(range(1, ntp), key=low_bit)

    def rs(c, d):
        return remote(rs_out.at[d, :, cols(c, rw)], rs_in.at[d, :, cols(c, rw)],
                      rs_s.at[c, d], rs_r.at[c, d], "tp", low_bit(d))

    def partial(c, d):
        value = tot[block(d), cols(c, rw)]
        for b in tp_bits:
            if d == 0 or b < low_bit(d):
                value = value + rs_in[d | b, :, cols(c, rw)].astype(jnp.float32)
        return value

    def rs_send(c, b):
        for d in rs_order:
            if low_bit(d) == b:
                rs_out[d, :, cols(c, rw)] = partial(c, d).astype(jnp.bfloat16)
                go(rs(c, d))

    def rs_wait(c, b):
        for d in rs_order:
            if low_bit(d) == b:
                rs(c, d).wait_recv()

    def tp_task():
        for c in range(RS_CHUNKS):
            tot[:, cols(c, rw)] = dot(grads[...], wcat[cols(c, rw), :], 1, 1)
            rs_send(c, 1)
        yield
        for b in tp_bits[1:]:
            for c in range(RS_CHUNKS):
                rs_wait(c, b // 2)
                rs_send(c, b)
        yield
        inner = jnp.zeros((rows, 1), jnp.float32)
        scale_back = inv_ref[:, 0:1]
        for c in range(RS_CHUNKS):
            rs_wait(c, tp_bits[-1])
            value = partial(c, 0)
            tot[block(0), cols(c, rw)] = value
            product = value * (x_ref[:, cols(c, rw)].astype(jnp.float32) * scale_back)
            gs[0, :, cols(c, rw)] = jnp.sum(product, axis=0, keepdims=True)
            inner = inner + jnp.sum(product * gain_ref[:, cols(c, rw)], axis=1, keepdims=True)
        rounds = [("tp", b) for b in tp_bits] + [("dp", b) for b in dp_bits]

        def exchange(k):
            axis, b = rounds[k]
            return remote(gs.at[k], gr.at[k], g_s.at[k], g_r.at[k], axis, b)

        go(exchange(0))
        inner = inner * (1.0 / width)
        for c in range(RS_CHUNKS):
            unit = x_ref[:, cols(c, rw)].astype(jnp.float32) * scale_back
            scaled = tot[block(0), cols(c, rw)] * gain_ref[:, cols(c, rw)]
            ig_ref[:, cols(c, rw)] = ((scaled - unit * inner) * scale_back).astype(jnp.bfloat16)
        for k in range(len(rounds)):
            yield
            exchange(k).wait_recv()
            if k + 1 < len(rounds):
                gs[k + 1] = gs[k] + gr[k]
                go(exchange(k + 1))
            else:
                gg_ref[...] = gs[k] + gr[k]

    task = tp_task()
    next(task)
    send_grads.wait_recv()
    for i in range(held):
        for d in range(0, ntp, 2):
            nx(i, d | 1).wait_recv()
    for q in range(DP_CHUNKS // 2):
        form(q)
    next(task)
    for q in range(DP_CHUNKS // 2, DP_CHUNKS):
        form(q)
    for step in range(DP_CHUNKS + LAGS[2]):
        for lag, stage in zip(LAGS, (gather, finish, end)):
            if 0 <= step - lag < DP_CHUNKS:
                stage(step - lag)
        if step >= TASK_AT and (step - TASK_AT) % 2 == 0:
            next(task, None)
    for _ in task:
        pass
    for copy in local:
        copy.wait()
    for copy in sends:
        copy.wait_send()
    for q in range(DP_CHUNKS):
        inward(q).wait_send()

    @pl.when(depth > 0)
    def _():
        for q in range(DP_CHUNKS):
            outward(q).wait_send()


def on_device(ntp, ndp, activations, cotangent, segment_ids, norm_gain, query_weight, key_value_weight):
    rows, width = activations.shape
    length, head = cotangent.shape
    angle = np.arange(length)[:, None] * 500000.0 ** (-np.arange(0, head, 2) / head)[None, :]
    cosine = np.concatenate([np.cos(angle), np.cos(angle)], axis=1).astype(np.float32)
    sine = np.concatenate([-np.sin(angle), np.sin(angle)], axis=1).astype(np.float32)
    nb = len(bits_of(ntp)) + len(bits_of(ndp))
    bf, f32 = jnp.bfloat16, jnp.float32
    vmem = pl.BlockSpec(memory_space=pltpu.VMEM)
    anywhere = pl.BlockSpec(memory_space=pl.ANY)
    hbm = pl.BlockSpec(memory_space=pltpu.HBM)
    dma = pltpu.SemaphoreType.DMA
    outs = pl.pallas_call(
        functools.partial(kernel, ntp, ndp),
        out_shape=[
            jax.ShapeDtypeStruct((rows, width), bf),
            jax.ShapeDtypeStruct((width, head), bf),
            jax.ShapeDtypeStruct((width, head), bf),
            jax.ShapeDtypeStruct((1, width), f32),
        ],
        in_specs=[hbm] * 8,
        out_specs=[vmem, anywhere, anywhere, vmem],
        scratch_shapes=[
            pltpu.VMEM((width, 2 * head), bf),
            pltpu.VMEM((length, width), bf),
            pltpu.VMEM((length, width // 2), bf),
            pltpu.VMEM((length, 2 * head), bf),
            pltpu.VMEM((length, 2 * head), bf),
            pltpu.VMEM((length, width), f32),
            pltpu.VMEM((ntp, rows, width), bf),
            pltpu.VMEM((ntp, rows, width), bf),
            pltpu.VMEM((width // 2, 2 * head), bf),
            pltpu.VMEM((DP_CHUNKS, 2, width // 2 // DP_CHUNKS, 2 * head), bf),
            pltpu.VMEM((width, 2 * head), bf),
            pltpu.VMEM((nb, 1, width), f32),
            pltpu.VMEM((nb, 1, width), f32),
            pltpu.VMEM((2, length, head), bf),
            pltpu.VMEM((2, length, head), bf),
            pltpu.VMEM((rows, 128), f32),
            dma((2,)),
            dma((DP_CHUNKS, 4)),
            dma((AG_CHUNKS, ntp)),
            dma((AG_CHUNKS, ntp)),
            dma((AG_CHUNKS // 2, ntp)),
            dma((AG_CHUNKS // 2, ntp)),
            dma,
            dma,
            dma((RS_CHUNKS, ntp)),
            dma((RS_CHUNKS, ntp)),
            dma((DP_CHUNKS,)),
            dma((DP_CHUNKS, 2)),
            dma((DP_CHUNKS,)),
            dma((DP_CHUNKS,)),
            dma((DP_CHUNKS,)),
            dma((DP_CHUNKS,)),
            dma((nb,)),
            dma((nb,)),
            dma((2,)),
            dma((2,)),
            pltpu.VMEM((rows, width), bf),
            pltpu.VMEM((length, head), bf),
            pltpu.VMEM((1, length), jnp.int32),
            pltpu.VMEM((1, width), f32),
            pltpu.VMEM((length, head), f32),
            pltpu.VMEM((length, head), f32),
            dma((6,)),
        ],
        compiler_params=pltpu.CompilerParams(
            collective_id=0, has_side_effects=True, vmem_limit_bytes=60 * 1024 * 1024),
    )(activations, cotangent, segment_ids.reshape(1, length), norm_gain.reshape(1, width),
      jnp.asarray(cosine), jnp.asarray(sine), query_weight, key_value_weight)
    return (outs[0], outs[1], outs[2], outs[3].reshape(width))


def solution(mesh):
    return jax.shard_map(
        functools.partial(on_device, mesh.shape["tp"], mesh.shape["dp"]),
        mesh=mesh,
        in_specs=(P(("dp", "tp"), None), P("dp", "tp"), P("dp"), P(), P(None, "tp"), P(None, "tp")),
        out_specs=(P(("dp", "tp"), None), P(None, "tp"), P(None, "tp"), P()),
        check_vma=False,
    )
```
